512 devices in a mesh: sta: 128 (over z_hi, y, x, core), cell: 4 (over z_lo).
Axes of the slice: x: 4, y: 8, z: 8 (z_hi: 2, z_lo: 4; z = z_hi * 4 + z_lo), core: 2. Of those that a mesh axis runs over, the one named last changes fastest.
Arguments:
- sensitivity: bfloat16 [2048, 52, 2048], P('sta', None, 'cell'), may hold values from -0.01953125 to 0.01953125
- footprint: int32 [128, 52], P('sta'), may hold values from 0 to 63, as said below
- linked: int32 [128, 9], P('sta'), may hold values from 0 to 1, as said below
- smooth_x: bfloat16 [16, 16], replicated, may hold values from 0 to 8, as said below
- smooth_y: bfloat16 [64, 64], replicated, may hold values from 0 to 8, as said below
- smooth_z: bfloat16 [128, 128], replicated, may hold values from 0 to 8, as said below
Outputs:
- band: float32 [2048, 144], P('sta', 'cell')
The draws below stay inside these ranges and needn't reach their ends.
Inputs may be any that keep to these rules, and one draw needn't show every extreme that they name: `footprint`: within a row the 52 tiles are different. linked[b, 4] is 1, and linked[b, 4 + k] equals linked[(b + k) mod the number of row blocks, 4 - k] for 1 <= k <= 4. `smooth_x`: Symmetric, with positive entries. `smooth_y`: Symmetric, with positive entries. `smooth_z`: Symmetric, with positive entries.
All inputs are finite; a program needn't handle non-finite values.
Results may differ from the reference program's by a relative error of at most 0.005.
Values may be sent and summed in bfloat16 or wider, within the bound.
A program may use at most 64 MiB of HBM per device.

```python
import math
import jax
import jax.numpy as jnp
from jax import lax

NX = 16
NY = 64
NZ = 128
TILE = 16
FOOT = 52
HALF = 4
ROWS_DEV = 16
TILES = 64
BAND = 9
ROWS = 2048
N_STA = 128


def smoothing_kernel(key, extent):
    key_length, key_rough = jax.random.split(key)
    length = jnp.exp(jax.random.uniform(key_length, (), jnp.float32, math.log(2.0), math.log(8.0)))
    places = jnp.arange(extent, dtype=jnp.float32)
    distance = jnp.abs(places[:, None] - places[None, :])
    roughness = jax.random.uniform(key_rough, (extent, extent), jnp.float32, 0.6, 1.4)
    roughness = 0.5 * (roughness + roughness.T)
    beside = jnp.where(distance > 0, jnp.exp(-distance / length) * roughness, 0.0)
    diagonal = jnp.sum(beside, axis=1) + 0.5
    kernel = (beside + jnp.diag(diagonal)) / jnp.sqrt(2.0 * length + 1.0)
    return kernel.astype(jnp.bfloat16)


def draw_smooth_x(key, part):
    return smoothing_kernel(jax.random.fold_in(key, 11), NX)


def draw_smooth_y(key, part):
    return smoothing_kernel(jax.random.fold_in(key, 12), NY)


def draw_smooth_z(key, part):
    return smoothing_kernel(jax.random.fold_in(key, 13), NZ)


def draw_footprint(key, part):
    keys = jax.random.split(jax.random.fold_in(key, 21), N_STA)
    orders = jax.vmap(lambda single: jax.random.permutation(single, TILES))(keys)
    return orders[:, :FOOT].astype(jnp.int32)


def draw_linked(key, part):
    key_density, key_scores = jax.random.split(jax.random.fold_in(key, 31))
    density = jax.random.randint(key_density, (N_STA, 1), 1, 5)
    scores = jax.random.randint(key_scores, (N_STA, HALF), 0, 4)
    upper_links = (scores < density).astype(jnp.int32)
    lower_links = [jnp.roll(upper_links[:, offset - 1], offset)[:, None] for offset in range(HALF, 0, -1)]
    middle = jnp.ones((N_STA, 1), jnp.int32)
    return jnp.concatenate(lower_links + [middle, upper_links], axis=1).astype(jnp.int32)


def steps_of(own_key, shape, cuts, smallest, largest):
    level = 1.0
    for axis_at, blocks in cuts:
        draws = jax.random.uniform(jax.random.fold_in(jax.random.fold_in(own_key, 6), axis_at), (blocks,), jnp.float32, smallest / len(cuts), largest / len(cuts))
        level = level * jnp.repeat(jnp.exp(draws), shape[axis_at] // blocks).reshape((-1,) + (1,) * (len(shape) - 1 - axis_at))
    return level


def normal_values(own_key, shape, deviation, reach, shards=(), kind=jnp.bfloat16):
    values = jax.random.normal(own_key, shape, jnp.float32) * deviation
    if len(shards) > 0:
        values = steps_of(own_key, shape, shards, -0.22, 0.18) * values
    return jnp.clip(values, min=-reach, max=reach).astype(kind)


def setup_inputs(seed: int = 0) -> dict:
    key_of = jax.random.split(jax.random.key(seed), 7)
    sensitivity = normal_values(key_of[0], (ROWS, FOOT, NZ * TILE), (FOOT * NZ * TILE) ** -0.5, 0.01953125, ((0, 128), (2, 4)))
    footprint = draw_footprint(jax.random.fold_in(key_of[6], 71), 0)
    linked = draw_linked(jax.random.fold_in(key_of[6], 71), 0)
    smooth_x = draw_smooth_x(jax.random.fold_in(key_of[6], 71), 0)
    smooth_y = draw_smooth_y(jax.random.fold_in(key_of[6], 71), 0)
    smooth_z = draw_smooth_z(jax.random.fold_in(key_of[6], 71), 0)
    return dict(sensitivity=sensitivity, footprint=footprint, linked=linked, smooth_x=smooth_x, smooth_y=smooth_y, smooth_z=smooth_z)


def spread_tiles(values, foot_tiles):
    onehot = (foot_tiles[:, None] == jnp.arange(TILES, dtype=jnp.int32)[None, :]).astype(jnp.float32)
    placed = jnp.einsum('rfk,ft->rtk', values.astype(jnp.float32), onehot)
    return placed.astype(jnp.bfloat16)


def smooth_depth(block, smooth_z):
    row_count, tile_count, slab_width = block.shape
    grid_field = block.reshape(row_count, tile_count, NZ, TILE).astype(jnp.float32)
    smoothed = jnp.einsum('rtzc,wz->rtwc', grid_field, smooth_z.astype(jnp.float32))
    return smoothed.astype(jnp.bfloat16).reshape(row_count, tile_count, slab_width)


def smooth_plane(field_rows, smooth_x, smooth_y):
    row_count, tile_count, slab_width = field_rows.shape
    blocks_along = tile_count // NX
    grid_field = field_rows.reshape(row_count, NX, blocks_along, NZ, TILE).astype(jnp.float32)
    across = jnp.einsum('rxbzc,vx->rvbzc', grid_field, smooth_x.astype(jnp.float32)).astype(jnp.bfloat16)
    y_kernel = smooth_y.astype(jnp.float32).reshape(blocks_along, TILE, blocks_along, TILE)
    along = jnp.einsum('rxbzc,ekbc->rxezk', across.astype(jnp.float32), y_kernel).astype(jnp.bfloat16)
    return along.reshape(row_count, tile_count, slab_width)


def reference(sensitivity, footprint, linked, smooth_x, smooth_y, smooth_z):
    blocks = sensitivity.reshape(N_STA, ROWS_DEV, FOOT, NZ * TILE)

    def one_block(index):
        values = blocks[index]
        depth_rows = smooth_depth(values, smooth_z)
        grid_rows = spread_tiles(depth_rows, footprint[index])
        smoothed = smooth_plane(grid_rows, smooth_x, smooth_y)

        def one_tile(column):
            other = (index + column - HALF) % N_STA
            picked = jnp.take(smoothed, footprint[other], axis=1).reshape(ROWS_DEV, FOOT * NZ * TILE)
            partner = blocks[other].reshape(ROWS_DEV, FOOT * NZ * TILE)
            product = jnp.dot(picked.astype(jnp.float32), partner.astype(jnp.float32).T, preferred_element_type=jnp.float32)
            return product * linked[index, column].astype(jnp.float32)

        band_parts = lax.map(one_tile, jnp.arange(BAND, dtype=jnp.int32))
        return jnp.transpose(band_parts, (1, 0, 2)).reshape(ROWS_DEV, BAND * ROWS_DEV)

    result = lax.map(one_block, jnp.arange(N_STA, dtype=jnp.int32))
    return result.reshape(ROWS, BAND * ROWS_DEV)
```

```python
import jax
import jax.numpy as jnp
from jax import lax
from jax.experimental import pallas as pl
from jax.experimental.pallas import tpu as pltpu
from jax.sharding import PartitionSpec as P

TILE = 16
FOOT = 52
TILES = 64
BAND = 9
ROWS = 16
WIDTH = 512
CELLS = 4
STAS = 128
PART = FOOT // CELLS
CHUNKS = ((0, 7), (7, 6))
SHARE = BAND * ROWS // CELLS
MESH = pl.DeviceIdType.MESH
OWN, BEHIND, BESIDE, ASIDE, FAR = range(5)
SLOTS = 5
F32, BF16 = jnp.float32, jnp.bfloat16


def iota(shape, dim):
    return lax.broadcasted_iota(jnp.int32, shape, dim)


def dot(a, b):
    return jnp.dot(a, b, preferred_element_type=F32)


def kron_rows(small_ref, wide_ref, big_ref):
    n = small_ref.shape[0]
    repeat = (iota((n, n * TILE), 0) == iota((n, n * TILE), 1) // TILE).astype(BF16)
    wide_ref[...] = dot(small_ref[...], repeat)
    same = iota((TILE, n * TILE), 0) == iota((TILE, n * TILE), 1) % TILE

    def row(a, carry):
        line = jnp.broadcast_to(wide_ref[pl.ds(a, 1), :], (TILE, n * TILE))
        big_ref[pl.ds(pl.multiple_of(a * TILE, TILE), TILE), :] = jnp.where(same, line, 0.0).astype(BF16)
        return carry

    lax.fori_loop(0, n, row, 0)


def kernel(
    x_hbm, inv_own, foot_own, inv_vmem, link, sx, sy, sz, out,
    held, tables, inv_smem, first, second, smoothed, wz, kx, ky, wide_z, wide_x,
    dense, across, field, square, turned, turned_in, shares, shares_in,
    z1_send, z1_recv, z2_send, z2_recv, h_send, h_recv, t_send, t_recv,
    b_send, b_recv, c_send, c_recv, local,
):
    s = lax.axis_index("sta")
    c = lax.axis_index("cell")
    odd = lax.rem(s, 2)

    def at(distance):
        return lax.rem(s + distance + STAS, STAS)

    def remote(src, dst, send, recv, sta, cell):
        return pltpu.make_async_remote_copy(
            src_ref=src, dst_ref=dst, send_sem=send, recv_sem=recv,
            device_id=(sta, cell), device_id_type=MESH,
        )

    sibling = s + 1 - 2 * odd
    aside_to = at(-3 + 2 * odd)

    barrier = pltpu.get_barrier_semaphore()
    for distance in (-4, -3, -2, -1, 1, 2, 3, 4):
        pl.semaphore_signal(barrier, inc=1, device_id=(at(distance), c), device_id_type=MESH)
    for j in (1, 2, 3):
        pl.semaphore_signal(barrier, inc=1, device_id=(s, lax.rem(c + j, CELLS)), device_id_type=MESH)
    pl.semaphore_wait(barrier, 11)

    def send_first(j, k):
        f0, fn = CHUNKS[k]
        to = lax.rem(c + j, CELLS)
        return remote(
            x_hbm.at[pl.ds(to * PART + f0, fn)], first.at[c, pl.ds(f0, fn)],
            z1_send.at[j - 1, k], z1_recv.at[j - 1, k], s, to,
        )

    def recv_first(j, k):
        f0, fn = CHUNKS[k]
        came = lax.rem(c + CELLS - j, CELLS)
        return remote(
            x_hbm.at[pl.ds(f0, fn)], first.at[came, pl.ds(f0, fn)],
            z1_send.at[j - 1, k], z1_recv.at[j - 1, k], s, came,
        )

    for k in range(len(CHUNKS)):
        for j in (2, 1, 3):
            send_first(j, k).start()

    def halo(slot, src, sta):
        return remote(src, held[slot].at[pl.ds(0, FOOT)], h_send.at[slot], h_recv.at[slot], sta, c)

    def table(slot, src, sta):
        return remote(src, tables[slot], t_send.at[slot], t_recv.at[slot], sta, c)

    sent_behind = halo(BEHIND, x_hbm, at(2))
    sent_behind.start()
    sent_table_behind = table(BEHIND, inv_vmem, at(2))
    sent_table_behind.start()
    sent_aside = halo(ASIDE, x_hbm, aside_to)
    sent_aside.start()
    sent_table_aside = table(ASIDE, inv_vmem, aside_to)
    sent_table_aside.start()

    own_first = pltpu.make_async_copy(x_hbm.at[pl.ds(c * PART, PART)], first.at[c], local.at[0])
    own_first.start()
    own_held = pltpu.make_async_copy(x_hbm, held[OWN].at[pl.ds(0, FOOT)], local.at[1])
    own_held.start()
    for slot in range(SLOTS):
        held[slot][FOOT] = jnp.zeros((ROWS, WIDTH), BF16)

    kron_rows(sx, wide_x, kx)
    wide = iota((TILES, WIDTH), 1)
    spread = (iota((TILES, WIDTH), 0) == (wide // 128) * TILE + wide % TILE).astype(BF16)
    rows_y = dot(sy[...], spread)
    level = (iota((TILE, WIDTH), 1) // TILE) % 8
    for b in range(4):
        for z in range(8):
            ky[(b * 8 + z) * TILE : (b * 8 + z + 1) * TILE, :] = jnp.where(
                level == z, rows_y[b * TILE : (b + 1) * TILE, :], 0.0
            ).astype(BF16)
    kron_rows(sz, wide_z, wz)

    def smooth_plane(slot, index):
        def along_x(b, carry):
            for x in range(16):
                dense[x * ROWS : (x + 1) * ROWS, :] = held[slot][index(b * 16 + x)]
            mixed = dot(kx[...], dense[...]).astype(BF16)
            for g in range(4):
                across[g, :, pl.ds(pl.multiple_of(b * 128, 128), 128)] = mixed[:, g * 128 : (g + 1) * 128]
            return carry

        lax.fori_loop(0, 4, along_x, 0)

        def along_y(g, carry):
            mixed = dot(across[g], ky[...]).astype(BF16)
            for e in range(4):
                field[
                    e * 16 : (e + 1) * 16, slot * ROWS : (slot + 1) * ROWS, pl.ds(pl.multiple_of(g * 128, 128), 128)
                ] = mixed[:, e * 128 : (e + 1) * 128].reshape(16, ROWS, 128)
            return carry

        lax.fori_loop(0, 4, along_y, 0)

    def take_table(slot):
        copy = pltpu.make_async_copy(tables[slot], inv_smem[slot], local.at[2 + slot])
        copy.start()
        copy.wait()

    own_held.wait()
    smooth_plane(OWN, lambda i: inv_own[0, i])

    def send_second(j, k):
        f0, fn = CHUNKS[k]
        to = lax.rem(c + j, CELLS)
        return remote(
            second.at[to, pl.ds(f0, fn)], smoothed.at[pl.ds(c * PART + f0, fn)],
            z2_send.at[j - 1, k], z2_recv.at[j - 1, k], s, to,
        )

    def recv_second(j, k):
        f0, fn = CHUNKS[k]
        came = lax.rem(c + CELLS - j, CELLS)
        return remote(
            second.at[came, pl.ds(f0, fn)], smoothed.at[pl.ds(came * PART + f0, fn)],
            z2_send.at[j - 1, k], z2_recv.at[j - 1, k], s, came,
        )

    def own_second(k):
        f0, fn = CHUNKS[k]
        return pltpu.make_async_copy(
            second.at[c, pl.ds(f0, fn)], smoothed.at[pl.ds(c * PART + f0, fn)], local.at[7 + k]
        )

    def smooth_depth(k):
        f0, fn = CHUNKS[k]
        for j in (1, 2, 3):
            recv_first(j, k).wait_recv()
        if k == 0:
            own_first.wait()
        rows = jnp.concatenate(
            [first[d, f0 : f0 + fn].reshape(fn * ROWS, WIDTH) for d in range(CELLS)], axis=1
        )
        for j in (2, 1, 3, 0):
            to = lax.rem(c + j, CELLS)
            done = dot(rows, wz[:, pl.ds(pl.multiple_of(to * WIDTH, WIDTH), WIDTH)])
            second[to, f0 : f0 + fn] = done.astype(BF16).reshape(fn, ROWS, WIDTH)
            if j:
                send_second(j, k).start()
            else:
                own_second(k).start()

    smooth_depth(0)

    halo(ASIDE, x_hbm, aside_to).wait_recv()
    table(ASIDE, inv_vmem, aside_to).wait_recv()
    take_table(ASIDE)
    smooth_plane(ASIDE, lambda i: inv_smem[ASIDE][0, i])

    halo(BEHIND, x_hbm, at(2)).wait_recv()
    table(BEHIND, inv_vmem, at(2)).wait_recv()
    came = held[BEHIND].at[pl.ds(0, FOOT)]
    sent_far = halo(FAR, came, at(2))
    sent_far.start()
    sent_table_far = table(FAR, tables[BEHIND], at(2))
    sent_table_far.start()
    sent_beside = halo(BESIDE, came, sibling)
    sent_beside.start()
    sent_table_beside = table(BESIDE, tables[BEHIND], sibling)
    sent_table_beside.start()
    take_table(BEHIND)
    smooth_plane(BEHIND, lambda i: inv_smem[BEHIND][0, i])

    smooth_depth(1)

    sent_beside.wait_recv()
    sent_table_beside.wait_recv()
    take_table(BESIDE)
    smooth_plane(BESIDE, lambda i: inv_smem[BESIDE][0, i])

    sent_far.wait_recv()
    sent_table_far.wait_recv()
    take_table(FAR)
    smooth_plane(FAR, lambda i: inv_smem[FAR][0, i])

    total = jnp.zeros((ROWS, SLOTS * ROWS), F32)
    for k, (f0, fn) in enumerate(CHUNKS):
        own_second(k).wait()
        for j in (1, 2, 3):
            recv_second(j, k).wait_recv()

        def product(e, total, f0=f0, fn=fn):
            for f in range(f0, f0 + fn):
                place = e * PART + f
                total = total + lax.dot_general(
                    smoothed[place], field[foot_own[0, place]],
                    (((1,), (1,)), ((), ())), preferred_element_type=F32,
                )
            return total

        total = lax.fori_loop(0, CELLS, product, total)

    square[...] = jnp.zeros((128, 128), F32)
    square[0:ROWS, 0 : SLOTS * ROWS] = total
    flipped = square[...].T
    back = {}
    for i, slot in enumerate((BEHIND, BESIDE, FAR, ASIDE)):
        turned[i] = flipped[slot * ROWS : (slot + 1) * ROWS, :]
    partners = (at(-2), at(-1 - 2 * odd), at(-4), at(1 + 2 * odd))
    for i in range(4):
        back[i] = remote(turned.at[i], turned_in.at[i], b_send.at[i], b_recv.at[i], partners[i], c)
        back[i].start()
    for i in range(4):
        back[i].wait_recv()

    def mine(slot):
        return total[:, slot * ROWS : (slot + 1) * ROWS]

    def theirs(i):
        return turned_in[i][:, :ROWS]

    is_odd = odd == 1
    beside, aside = mine(BESIDE), mine(ASIDE)
    parts = [
        mine(FAR),
        jnp.where(is_odd, beside, theirs(3)),
        mine(BEHIND),
        jnp.where(is_odd, theirs(3), beside),
        mine(OWN),
        jnp.where(is_odd, theirs(1), aside),
        theirs(0),
        jnp.where(is_odd, aside, theirs(1)),
        theirs(2),
    ]
    whole = jnp.concatenate(parts, axis=1) * link[0:1, 0 : BAND * ROWS]
    for e in range(CELLS):
        shares[e, :, 0:SHARE] = whole[:, e * SHARE : (e + 1) * SHARE]
    given = []
    for j in (1, 2, 3):
        to = lax.rem(c + j, CELLS)
        copy = remote(shares.at[to], shares_in.at[j - 1], c_send.at[j - 1], c_recv.at[j - 1], s, to)
        copy.start()
        given.append(copy)
    for copy in given:
        copy.wait_recv()
    summed = shares[c] + shares_in[0] + shares_in[1] + shares_in[2]
    out[...] = summed[:, 0:SHARE]

    for k in range(len(CHUNKS)):
        for j in (1, 2, 3):
            send_first(j, k).wait_send()
            send_second(j, k).wait_send()
    for copy in (
        sent_behind, sent_table_behind, sent_aside, sent_table_aside,
        sent_far, sent_table_far, sent_beside, sent_table_beside,
        *back.values(), *given,
    ):
        copy.wait_send()


def body(sensitivity, footprint, linked, smooth_x, smooth_y, smooth_z):
    values = jnp.transpose(sensitivity, (1, 0, 2))
    tiles = jnp.arange(TILES, dtype=jnp.int32)
    tile_of = (tiles % 16) * 4 + tiles // 16
    match = footprint[0][None, :] == tile_of[:, None]
    order = jnp.arange(FOOT, dtype=jnp.int32)[None, :]
    inverse = FOOT + jnp.sum(jnp.where(match, order - FOOT, 0), axis=1)
    inverse = jnp.broadcast_to(jnp.pad(inverse, (0, 128 - TILES))[None, :], (8, 128))
    foot = (footprint % 4) * 16 + footprint // 4
    link = jnp.repeat(linked.astype(F32), ROWS, axis=1)
    n_k = len(CHUNKS)
    vmem = pl.BlockSpec(memory_space=pltpu.VMEM)
    smem = pl.BlockSpec(memory_space=pltpu.SMEM)
    dma = pltpu.SemaphoreType.DMA
    return pl.pallas_call(
        kernel,
        out_shape=jax.ShapeDtypeStruct((ROWS, SHARE), F32),
        in_specs=[pl.BlockSpec(memory_space=pl.ANY), smem, smem, vmem, vmem, vmem, vmem, vmem],
        out_specs=vmem,
        scratch_shapes=[
            [pltpu.VMEM((FOOT + 1, ROWS, WIDTH), BF16)] * SLOTS,
            [pltpu.VMEM((8, 128), jnp.int32)] * SLOTS,
            [pltpu.SMEM((8, 128), jnp.int32)] * SLOTS,
            pltpu.VMEM((CELLS, PART, ROWS, WIDTH), BF16),
            pltpu.VMEM((CELLS, PART, ROWS, WIDTH), BF16),
            pltpu.VMEM((FOOT, ROWS, WIDTH), BF16),
            pltpu.VMEM((2048, 2048), BF16),
            pltpu.VMEM((256, 256), BF16),
            pltpu.VMEM((512, 512), BF16),
            pltpu.VMEM((128, 2048), F32),
            pltpu.VMEM((16, 256), F32),
            pltpu.VMEM((256, WIDTH), BF16),
            pltpu.VMEM((4, 256, WIDTH), BF16),
            pltpu.VMEM((TILES, SLOTS * ROWS, WIDTH), BF16),
            pltpu.VMEM((128, 128), F32),
            pltpu.VMEM((4, ROWS, 128), F32),
            pltpu.VMEM((4, ROWS, 128), F32),
            pltpu.VMEM((CELLS, ROWS, 128), F32),
            pltpu.VMEM((CELLS - 1, ROWS, 128), F32),
            dma((3, n_k)), dma((3, n_k)), dma((3, n_k)), dma((3, n_k)),
            dma((SLOTS,)), dma((SLOTS,)), dma((SLOTS,)), dma((SLOTS,)),
            dma((4,)), dma((4,)), dma((3,)), dma((3,)), dma((10,)),
        ],
        compiler_params=pltpu.CompilerParams(
            collective_id=0, has_side_effects=True, vmem_limit_bytes=56 * 2**20
        ),
        name="band",
    )(values, inverse, foot, inverse, link, smooth_x, smooth_y, smooth_z)


def solution(mesh):
    return jax.shard_map(
        body,
        mesh=mesh,
        in_specs=(P("sta", None, "cell"), P("sta", None), P("sta", None), P(), P(), P()),
        out_specs=P("sta", "cell"),
        check_vma=False,
    )
```

```python
import jax
import jax.numpy as jnp
from jax import lax
from jax.experimental import pallas as pl
from jax.experimental.pallas import tpu as pltpu
from jax.sharding import PartitionSpec as P

TILE = 16
FOOT = 52
TILES = 64
BAND = 9
ROWS = 16
WIDTH = 512
CELLS = 4
STAS = 128
PART = FOOT // CELLS
CHUNKS = ((0, 7), (7, 6))
SHARE = BAND * ROWS // CELLS
MESH = pl.DeviceIdType.MESH
OWN, BEHIND, BESIDE, ASIDE, FAR = range(5)
SLOTS = 5
F32, BF16 = jnp.float32, jnp.bfloat16
PIECES = {BEHIND: 4, BESIDE: 1, ASIDE: 2, FAR: 4}
HALF_STAS = 64


def crossings():
    flows = []
    for k in range(2):
        for slot, source, column in ((BEHIND, 62 + k, k), (FAR, 60 + k, 2 + k)):
            flows.append((slot, 0, source, None, k))
            for p, row in enumerate((1, 7, 6), 1):
                flows.append((slot, p, source, 8 * row + column, k))
    for source, relay, target in ((0, 53, 61), (2, 52, 63)):
        flows.append((ASIDE, 0, source, None, target))
        flows.append((ASIDE, 1, source, relay, target))
    return flows


FLOWS = crossings()
SOURCES = sorted({flow[2] for flow in FLOWS})
RELAYED = [flow for flow in FLOWS if flow[3] is not None]


def iota(shape, dim):
    return lax.broadcasted_iota(jnp.int32, shape, dim)


def dot(a, b):
    return jnp.dot(a, b, preferred_element_type=F32)


def kron_rows(small_ref, wide_ref, big_ref):
    n = small_ref.shape[0]
    repeat = (iota((n, n * TILE), 0) == iota((n, n * TILE), 1) // TILE).astype(BF16)
    wide_ref[...] = dot(small_ref[...], repeat)
    same = iota((TILE, n * TILE), 0) == iota((TILE, n * TILE), 1) % TILE

    def row(a, carry):
        line = jnp.broadcast_to(wide_ref[pl.ds(a, 1), :], (TILE, n * TILE))
        big_ref[pl.ds(pl.multiple_of(a * TILE, TILE), TILE), :] = jnp.where(same, line, 0.0).astype(BF16)
        return carry

    lax.fori_loop(0, n, row, 0)


def kernel(
    x_hbm, inv_own, foot_own, inv_vmem, link, sx, sy, sz, out,
    held, tables, inv_smem, first, second, smoothed, wz, kx, ky, wide_z, wide_x,
    dense, across, field, square, turned, turned_in, shares, shares_in,
    z1_send, z1_recv, z2_send, z2_recv, h_send, h_recv, t_send, t_recv,
    b_send, b_recv, c_send, c_recv, local, relay, cross_send, relay_send, relay_recv,
):
    s = lax.axis_index("sta")
    c = lax.axis_index("cell")
    odd = lax.rem(s, 2)

    def at(distance):
        return lax.rem(s + distance + STAS, STAS)

    def remote(src, dst, send, recv, sta, cell):
        return pltpu.make_async_remote_copy(
            src_ref=src, dst_ref=dst, send_sem=send, recv_sem=recv,
            device_id=(sta, cell), device_id_type=MESH,
        )

    sibling = s + 1 - 2 * odd
    aside_to = at(-3 + 2 * odd)
    place = lax.rem(s, HALF_STAS)
    here = s - place
    beyond = HALF_STAS - here

    barrier = pltpu.get_barrier_semaphore()
    for distance in (-4, -3, -2, -1, 1, 2, 3, 4):
        pl.semaphore_signal(barrier, inc=1, device_id=(at(distance), c), device_id_type=MESH)
    for j in (1, 2, 3):
        pl.semaphore_signal(barrier, inc=1, device_id=(s, lax.rem(c + j, CELLS)), device_id_type=MESH)
    for slot, p, source, relay_at, target in RELAYED:
        @pl.when(place == relay_at)
        def _(source=source):
            pl.semaphore_signal(barrier, inc=1, device_id=(beyond + source, c), device_id_type=MESH)

        @pl.when(place == target)
        def _(relay_at=relay_at):
            pl.semaphore_signal(barrier, inc=1, device_id=(here + relay_at, c), device_id_type=MESH)

    greeted = jnp.int32(11)
    for slot, p, source, relay_at, target in RELAYED:
        greeted += jnp.where(jnp.logical_or(place == relay_at, place == source), 1, 0)
    pl.semaphore_wait(barrier, greeted)

    def send_first(j, k):
        f0, fn = CHUNKS[k]
        to = lax.rem(c + j, CELLS)
        return remote(
            x_hbm.at[pl.ds(to * PART + f0, fn)], first.at[c, pl.ds(f0, fn)],
            z1_send.at[j - 1, k], z1_recv.at[j - 1, k], s, to,
        )

    def recv_first(j, k):
        f0, fn = CHUNKS[k]
        came = lax.rem(c + CELLS - j, CELLS)
        return remote(
            x_hbm.at[pl.ds(f0, fn)], first.at[came, pl.ds(f0, fn)],
            z1_send.at[j - 1, k], z1_recv.at[j - 1, k], s, came,
        )

    for k in range(len(CHUNKS)):
        for j in (2, 1, 3):
            send_first(j, k).start()

    def cut(slot, p):
        size = FOOT // PIECES[slot]
        return pl.ds(p * size, size)

    def halo(slot, p, src, send, sta):
        return remote(src.at[cut(slot, p)], held[slot].at[cut(slot, p)], send, h_recv.at[slot, p], sta, c)

    def halos(slot, src, sta):
        return [halo(slot, p, src, h_send.at[slot, p], sta) for p in range(PIECES[slot])]

    def begin(copies):
        for copy in copies:
            copy.start()

    def to_relay(slot, p, send, sta):
        size = FOOT // PIECES[slot]
        return remote(x_hbm.at[cut(slot, p)], relay.at[pl.ds(0, size)], send, relay_recv.at[0], sta, c)

    def from_relay(slot, p, sta):
        size = FOOT // PIECES[slot]
        return remote(
            relay.at[pl.ds(0, size)], held[slot].at[cut(slot, p)], relay_send.at[0], h_recv.at[slot, p], sta, c
        )

    def table(slot, sta):
        return remote(inv_vmem, tables[slot], t_send.at[slot], t_recv.at[slot], sta, c)

    sent_tables = [
        table(BEHIND, at(2)), table(BESIDE, at(3 - 2 * odd)), table(ASIDE, aside_to), table(FAR, at(4))
    ]
    begin(sent_tables)
    sent_behind = halos(BEHIND, x_hbm, at(2))
    sent_aside = halos(ASIDE, x_hbm, aside_to)
    inner = place < 62
    straight = jnp.logical_and(place != 0, place != 2)

    @pl.when(inner)
    def _():
        begin(sent_behind)

    @pl.when(straight)
    def _():
        begin(sent_aside)

    for source_at in SOURCES:
        @pl.when(place == source_at)
        def _(source_at=source_at):
            for slot, p, source, relay_at, target in FLOWS:
                if source == source_at:
                    send = cross_send.at[p] if slot == FAR else h_send.at[slot, p]
                    if relay_at is None:
                        halo(slot, p, x_hbm, send, beyond + target).start()
                    else:
                        to_relay(slot, p, send, beyond + relay_at).start()

    own_first = pltpu.make_async_copy(x_hbm.at[pl.ds(c * PART, PART)], first.at[c], local.at[0])
    own_first.start()
    own_held = pltpu.make_async_copy(x_hbm, held[OWN].at[pl.ds(0, FOOT)], local.at[1])
    own_held.start()
    for slot in range(SLOTS):
        held[slot][FOOT] = jnp.zeros((ROWS, WIDTH), BF16)

    kron_rows(sx, wide_x, kx)
    wide = iota((TILES, WIDTH), 1)
    spread = (iota((TILES, WIDTH), 0) == (wide // 128) * TILE + wide % TILE).astype(BF16)
    rows_y = dot(sy[...], spread)
    level = (iota((TILE, WIDTH), 1) // TILE) % 8
    for b in range(4):
        for z in range(8):
            ky[(b * 8 + z) * TILE : (b * 8 + z + 1) * TILE, :] = jnp.where(
                level == z, rows_y[b * TILE : (b + 1) * TILE, :], 0.0
            ).astype(BF16)
    kron_rows(sz, wide_z, wz)

    def smooth_plane(slot, index):
        def along_x(b, carry):
            for x in range(16):
                dense[x * ROWS : (x + 1) * ROWS, :] = held[slot][index(b * 16 + x)]
            mixed = dot(kx[...], dense[...]).astype(BF16)
            for g in range(4):
                across[g, :, pl.ds(pl.multiple_of(b * 128, 128), 128)] = mixed[:, g * 128 : (g + 1) * 128]
            return carry

        lax.fori_loop(0, 4, along_x, 0)

        def along_y(g, carry):
            mixed = dot(across[g], ky[...]).astype(BF16)
            for e in range(4):
                field[
                    e * 16 : (e + 1) * 16, slot * ROWS : (slot + 1) * ROWS, pl.ds(pl.multiple_of(g * 128, 128), 128)
                ] = mixed[:, e * 128 : (e + 1) * 128].reshape(16, ROWS, 128)
            return carry

        lax.fori_loop(0, 4, along_y, 0)

    def take_table(slot):
        copy = pltpu.make_async_copy(tables[slot], inv_smem[slot], local.at[2 + slot])
        copy.start()
        copy.wait()

    own_held.wait()
    smooth_plane(OWN, lambda i: inv_own[0, i])

    def send_second(j, k):
        f0, fn = CHUNKS[k]
        to = lax.rem(c + j, CELLS)
        return remote(
            second.at[to, pl.ds(f0, fn)], smoothed.at[pl.ds(c * PART + f0, fn)],
            z2_send.at[j - 1, k], z2_recv.at[j - 1, k], s, to,
        )

    def recv_second(j, k):
        f0, fn = CHUNKS[k]
        came = lax.rem(c + CELLS - j, CELLS)
        return remote(
            second.at[came, pl.ds(f0, fn)], smoothed.at[pl.ds(came * PART + f0, fn)],
            z2_send.at[j - 1, k], z2_recv.at[j - 1, k], s, came,
        )

    def own_second(k):
        f0, fn = CHUNKS[k]
        return pltpu.make_async_copy(
            second.at[c, pl.ds(f0, fn)], smoothed.at[pl.ds(c * PART + f0, fn)], local.at[7 + k]
        )

    def smooth_depth(k):
        f0, fn = CHUNKS[k]
        for j in (1, 2, 3):
            recv_first(j, k).wait_recv()
        if k == 0:
            own_first.wait()
        rows = jnp.concatenate(
            [first[d, f0 : f0 + fn].reshape(fn * ROWS, WIDTH) for d in range(CELLS)], axis=1
        )
        for j in (2, 1, 3, 0):
            to = lax.rem(c + j, CELLS)
            done = dot(rows, wz[:, pl.ds(pl.multiple_of(to * WIDTH, WIDTH), WIDTH)])
            second[to, f0 : f0 + fn] = done.astype(BF16).reshape(fn, ROWS, WIDTH)
            if j:
                send_second(j, k).start()
            else:
                own_second(k).start()

    smooth_depth(0)

    for p in range(PIECES[ASIDE]):
        sent_aside[p].wait_recv()
    sent_tables[2].wait_recv()
    take_table(ASIDE)
    smooth_plane(ASIDE, lambda i: inv_smem[ASIDE][0, i])

    for slot, p, source, relay_at, target in RELAYED:
        @pl.when(place == relay_at)
        def _(slot=slot, p=p, source=source, target=target):
            to_relay(slot, p, h_send.at[BEHIND, 0], beyond + source).wait_recv()
            from_relay(slot, p, here + target).start()

    sent_far = halos(FAR, held[BEHIND], at(2))
    for p in range(PIECES[BEHIND]):
        sent_behind[p].wait_recv()

        @pl.when(inner)
        def _(p=p):
            sent_far[p].start()

    sent_beside = halos(BESIDE, held[BEHIND], sibling)
    begin(sent_beside)
    sent_tables[0].wait_recv()
    take_table(BEHIND)
    smooth_plane(BEHIND, lambda i: inv_smem[BEHIND][0, i])

    smooth_depth(1)

    sent_beside[0].wait_recv()
    sent_tables[1].wait_recv()
    take_table(BESIDE)
    smooth_plane(BESIDE, lambda i: inv_smem[BESIDE][0, i])

    for p in range(PIECES[FAR]):
        sent_far[p].wait_recv()
    sent_tables[3].wait_recv()
    take_table(FAR)
    smooth_plane(FAR, lambda i: inv_smem[FAR][0, i])

    total = jnp.zeros((ROWS, SLOTS * ROWS), F32)
    for k, (f0, fn) in enumerate(CHUNKS):
        own_second(k).wait()
        for j in (1, 2, 3):
            recv_second(j, k).wait_recv()

        def product(e, total, f0=f0, fn=fn):
            for f in range(f0, f0 + fn):
                place = e * PART + f
                total = total + lax.dot_general(
                    smoothed[place], field[foot_own[0, place]],
                    (((1,), (1,)), ((), ())), preferred_element_type=F32,
                )
            return total

        total = lax.fori_loop(0, CELLS, product, total)

    square[...] = jnp.zeros((128, 128), F32)
    square[0:ROWS, 0 : SLOTS * ROWS] = total
    flipped = square[...].T
    back = {}
    for i, slot in enumerate((BEHIND, BESIDE, FAR, ASIDE)):
        turned[i] = flipped[slot * ROWS : (slot + 1) * ROWS, :]
    partners = (at(-2), at(-1 - 2 * odd), at(-4), at(1 + 2 * odd))
    for i in range(4):
        back[i] = remote(turned.at[i], turned_in.at[i], b_send.at[i], b_recv.at[i], partners[i], c)
        back[i].start()
    for i in range(4):
        back[i].wait_recv()

    def mine(slot):
        return total[:, slot * ROWS : (slot + 1) * ROWS]

    def theirs(i):
        return turned_in[i][:, :ROWS]

    is_odd = odd == 1
    beside, aside = mine(BESIDE), mine(ASIDE)
    parts = [
        mine(FAR),
        jnp.where(is_odd, beside, theirs(3)),
        mine(BEHIND),
        jnp.where(is_odd, theirs(3), beside),
        mine(OWN),
        jnp.where(is_odd, theirs(1), aside),
        theirs(0),
        jnp.where(is_odd, aside, theirs(1)),
        theirs(2),
    ]
    whole = jnp.concatenate(parts, axis=1) * link[0:1, 0 : BAND * ROWS]
    for e in range(CELLS):
        shares[e, :, 0:SHARE] = whole[:, e * SHARE : (e + 1) * SHARE]
    given = []
    for j in (1, 2, 3):
        to = lax.rem(c + j, CELLS)
        copy = remote(shares.at[to], shares_in.at[j - 1], c_send.at[j - 1], c_recv.at[j - 1], s, to)
        copy.start()
        given.append(copy)
    for copy in given:
        copy.wait_recv()
    summed = shares[c] + shares_in[0] + shares_in[1] + shares_in[2]
    out[...] = summed[:, 0:SHARE]

    for k in range(len(CHUNKS)):
        for j in (1, 2, 3):
            send_first(j, k).wait_send()
            send_second(j, k).wait_send()
    for copy in (*sent_tables, *sent_behind, *sent_aside, *sent_beside, *back.values(), *given):
        copy.wait_send()

    @pl.when(inner)
    def _():
        for copy in sent_far:
            copy.wait_send()

    @pl.when(jnp.logical_or(place == 60, place == 61))
    def _():
        for p in range(PIECES[FAR]):
            halo(FAR, p, x_hbm, cross_send.at[p], beyond).wait_send()

    for slot, p, source, relay_at, target in RELAYED:
        @pl.when(place == relay_at)
        def _(slot=slot, p=p, target=target):
            from_relay(slot, p, here + target).wait_send()


def body(sensitivity, footprint, linked, smooth_x, smooth_y, smooth_z):
    values = jnp.transpose(sensitivity, (1, 0, 2))
    tiles = jnp.arange(TILES, dtype=jnp.int32)
    tile_of = (tiles % 16) * 4 + tiles // 16
    match = footprint[0][None, :] == tile_of[:, None]
    order = jnp.arange(FOOT, dtype=jnp.int32)[None, :]
    inverse = FOOT + jnp.sum(jnp.where(match, order - FOOT, 0), axis=1)
    inverse = jnp.broadcast_to(jnp.pad(inverse, (0, 128 - TILES))[None, :], (8, 128))
    foot = (footprint % 4) * 16 + footprint // 4
    link = jnp.repeat(linked.astype(F32), ROWS, axis=1)
    n_k = len(CHUNKS)
    vmem = pl.BlockSpec(memory_space=pltpu.VMEM)
    smem = pl.BlockSpec(memory_space=pltpu.SMEM)
    dma = pltpu.SemaphoreType.DMA
    return pl.pallas_call(
        kernel,
        out_shape=jax.ShapeDtypeStruct((ROWS, SHARE), F32),
        in_specs=[pl.BlockSpec(memory_space=pl.ANY), smem, smem, vmem, vmem, vmem, vmem, vmem],
        out_specs=vmem,
        scratch_shapes=[
            [pltpu.VMEM((FOOT + 1, ROWS, WIDTH), BF16)] * SLOTS,
            [pltpu.VMEM((8, 128), jnp.int32)] * SLOTS,
            [pltpu.SMEM((8, 128), jnp.int32)] * SLOTS,
            pltpu.VMEM((CELLS, PART, ROWS, WIDTH), BF16),
            pltpu.VMEM((CELLS, PART, ROWS, WIDTH), BF16),
            pltpu.VMEM((FOOT, ROWS, WIDTH), BF16),
            pltpu.VMEM((2048, 2048), BF16),
            pltpu.VMEM((256, 256), BF16),
            pltpu.VMEM((512, 512), BF16),
            pltpu.VMEM((128, 2048), F32),
            pltpu.VMEM((16, 256), F32),
            pltpu.VMEM((256, WIDTH), BF16),
            pltpu.VMEM((4, 256, WIDTH), BF16),
            pltpu.VMEM((TILES, SLOTS * ROWS, WIDTH), BF16),
            pltpu.VMEM((128, 128), F32),
            pltpu.VMEM((4, ROWS, 128), F32),
            pltpu.VMEM((4, ROWS, 128), F32),
            pltpu.VMEM((CELLS, ROWS, 128), F32),
            pltpu.VMEM((CELLS - 1, ROWS, 128), F32),
            dma((3, n_k)), dma((3, n_k)), dma((3, n_k)), dma((3, n_k)),
            dma((SLOTS, 4)), dma((SLOTS, 4)), dma((SLOTS,)), dma((SLOTS,)),
            dma((4,)), dma((4,)), dma((3,)), dma((3,)), dma((10,)),
            pltpu.VMEM((FOOT // 2, ROWS, WIDTH), BF16), dma((4,)), dma((1,)), dma((1,)),
        ],
        compiler_params=pltpu.CompilerParams(
            collective_id=0, has_side_effects=True, vmem_limit_bytes=56 * 2**20
        ),
        name="band",
    )(values, inverse, foot, inverse, link, smooth_x, smooth_y, smooth_z)


def solution(mesh):
    return jax.shard_map(
        body,
        mesh=mesh,
        in_specs=(P("sta", None, "cell"), P("sta", None), P("sta", None), P(), P(), P()),
        out_specs=P("sta", "cell"),
        check_vma=False,
    )
```

```python
import jax
import jax.numpy as jnp
from jax import lax
from jax.experimental import pallas as pl
from jax.experimental.pallas import tpu as pltpu
from jax.sharding import PartitionSpec as P

TILE = 16
FOOT = 52
TILES = 64
BAND = 9
ROWS = 16
WIDTH = 512
CELLS = 4
STAS = 128
PART = FOOT // CELLS
CHUNKS = ((0, 7), (7, 6))
SHARE = BAND * ROWS // CELLS
MESH = pl.DeviceIdType.MESH
OWN, BEHIND, BESIDE, ASIDE, FAR = range(5)
SLOTS = 5
F32, BF16 = jnp.float32, jnp.bfloat16
PIECES = {BEHIND: 4, BESIDE: 1, ASIDE: 2, FAR: 4}
HALF_STAS = 64


def crossings():
    flows = []
    for slot, source, column, target in ((BEHIND, 62, 0, 0), (BEHIND, 63, 1, 1), (FAR, 61, 3, 1)):
        flows.append((slot, 0, source, None, target))
        for p, row in enumerate((1, 7, 6), 1):
            flows.append((slot, p, source, 8 * row + column, target))
    for source, relay, target in ((0, 53, 61), (2, 52, 63)):
        flows.append((ASIDE, 0, source, None, target))
        flows.append((ASIDE, 1, source, relay, target))
    return flows


FLOWS = crossings()
SOURCES = sorted({flow[2] for flow in FLOWS})
RELAYED = [flow for flow in FLOWS if flow[3] is not None]


def iota(shape, dim):
    return lax.broadcasted_iota(jnp.int32, shape, dim)


def dot(a, b):
    return jnp.dot(a, b, preferred_element_type=F32)


def kron_rows(small_ref, wide_ref, big_ref):
    n = small_ref.shape[0]
    repeat = (iota((n, n * TILE), 0) == iota((n, n * TILE), 1) // TILE).astype(BF16)
    wide_ref[...] = dot(small_ref[...], repeat)
    same = iota((TILE, n * TILE), 0) == iota((TILE, n * TILE), 1) % TILE

    def row(a, carry):
        line = jnp.broadcast_to(wide_ref[pl.ds(a, 1), :], (TILE, n * TILE))
        big_ref[pl.ds(pl.multiple_of(a * TILE, TILE), TILE), :] = jnp.where(same, line, 0.0).astype(BF16)
        return carry

    lax.fori_loop(0, n, row, 0)


def kernel(
    x_hbm, inv_own, foot_own, inv_vmem, link, sx, sy, sz, out,
    held, tables, inv_smem, first, second, smoothed, wz, kx, ky, wide_z, wide_x,
    dense, across, field, square, turned, turned_in, shares, shares_in,
    z1_send, z1_recv, z2_send, z2_recv, h_send, h_recv, t_send, t_recv,
    b_send, b_recv, c_send, c_recv, local, relay, cross_send, relay_send, relay_recv,
    hop, hop_send, hop_recv, over_send,
):
    s = lax.axis_index("sta")
    c = lax.axis_index("cell")
    odd = lax.rem(s, 2)

    def at(distance):
        return lax.rem(s + distance + STAS, STAS)

    def remote(src, dst, send, recv, sta, cell):
        return pltpu.make_async_remote_copy(
            src_ref=src, dst_ref=dst, send_sem=send, recv_sem=recv,
            device_id=(sta, cell), device_id_type=MESH,
        )

    sibling = s + 1 - 2 * odd
    aside_to = at(-3 + 2 * odd)
    place = lax.rem(s, HALF_STAS)
    here = s - place
    beyond = HALF_STAS - here

    barrier = pltpu.get_barrier_semaphore()
    for distance in (-4, -3, -2, -1, 1, 2, 3, 4):
        pl.semaphore_signal(barrier, inc=1, device_id=(at(distance), c), device_id_type=MESH)
    for j in (1, 2, 3):
        pl.semaphore_signal(barrier, inc=1, device_id=(s, lax.rem(c + j, CELLS)), device_id_type=MESH)
    for slot, p, source, relay_at, target in RELAYED:
        @pl.when(place == relay_at)
        def _(source=source):
            pl.semaphore_signal(barrier, inc=1, device_id=(beyond + source, c), device_id_type=MESH)

        @pl.when(place == target)
        def _(relay_at=relay_at):
            pl.semaphore_signal(barrier, inc=1, device_id=(here + relay_at, c), device_id_type=MESH)

    greeted = jnp.int32(11)
    for slot, p, source, relay_at, target in RELAYED:
        greeted += jnp.where(jnp.logical_or(place == relay_at, place == source), 1, 0)
    pl.semaphore_wait(barrier, greeted)

    def send_first(j, k):
        f0, fn = CHUNKS[k]
        to = lax.rem(c + j, CELLS)
        return remote(
            x_hbm.at[pl.ds(to * PART + f0, fn)], first.at[c, pl.ds(f0, fn)],
            z1_send.at[j - 1, k], z1_recv.at[j - 1, k], s, to,
        )

    def recv_first(j, k):
        f0, fn = CHUNKS[k]
        came = lax.rem(c + CELLS - j, CELLS)
        return remote(
            x_hbm.at[pl.ds(f0, fn)], first.at[came, pl.ds(f0, fn)],
            z1_send.at[j - 1, k], z1_recv.at[j - 1, k], s, came,
        )

    for k in range(len(CHUNKS)):
        for j in (2, 1, 3):
            send_first(j, k).start()

    def cut(slot, p):
        size = FOOT // PIECES[slot]
        return pl.ds(p * size, size)

    def halo(slot, p, src, send, sta):
        return remote(src.at[cut(slot, p)], held[slot].at[cut(slot, p)], send, h_recv.at[slot, p], sta, c)

    def halos(slot, src, sta):
        return [halo(slot, p, src, h_send.at[slot, p], sta) for p in range(PIECES[slot])]

    def begin(copies):
        for copy in copies:
            copy.start()

    def to_relay(slot, p, send, sta):
        size = FOOT // PIECES[slot]
        return remote(x_hbm.at[cut(slot, p)], relay.at[pl.ds(0, size)], send, relay_recv.at[0], sta, c)

    def from_relay(slot, p, sta):
        size = FOOT // PIECES[slot]
        return remote(
            relay.at[pl.ds(0, size)], held[slot].at[cut(slot, p)], relay_send.at[0], h_recv.at[slot, p], sta, c
        )

    def table(slot, sta):
        return remote(inv_vmem, tables[slot], t_send.at[slot], t_recv.at[slot], sta, c)

    sent_tables = [
        table(BEHIND, at(2)), table(BESIDE, at(3 - 2 * odd)), table(ASIDE, aside_to), table(FAR, at(8 * odd - 4))
    ]
    begin(sent_tables)
    sent_behind = halos(BEHIND, x_hbm, at(2))
    sent_aside = halos(ASIDE, x_hbm, aside_to)
    sent_far = halos(FAR, held[BEHIND], at(2))
    over_far = [halo(FAR, p, held[ASIDE], over_send.at[p], sibling) for p in range(PIECES[FAR])]
    sent_beside = halos(BESIDE, held[BEHIND], sibling)
    inner = place < 62
    is_odd = odd == 1
    hopping = jnp.logical_and(odd == 0, place >= 4)
    hops = jnp.logical_and(odd == 0, jnp.logical_and(place >= 2, place <= 60))
    sent_hop = [
        remote(x_hbm.at[cut(ASIDE, p)], hop.at[cut(ASIDE, p)], h_send.at[ASIDE, p], hop_recv.at[p], at(-2), c)
        for p in range(PIECES[ASIDE])
    ]
    past_hop = [halo(ASIDE, p, hop, hop_send.at[p], at(-1)) for p in range(PIECES[ASIDE])]

    @pl.when(inner)
    def _():
        begin(sent_behind)

    @pl.when(is_odd)
    def _():
        begin(sent_aside)

    @pl.when(hopping)
    def _():
        begin(sent_hop)

    for source_at in SOURCES:
        @pl.when(place == source_at)
        def _(source_at=source_at):
            for slot, p, source, relay_at, target in FLOWS:
                if source == source_at:
                    send = cross_send.at[p] if slot == FAR else h_send.at[slot, p]
                    if relay_at is None:
                        halo(slot, p, x_hbm, send, beyond + target).start()
                    else:
                        to_relay(slot, p, send, beyond + relay_at).start()

    own_first = pltpu.make_async_copy(x_hbm.at[pl.ds(c * PART, PART)], first.at[c], local.at[0])
    own_first.start()
    own_held = pltpu.make_async_copy(x_hbm, held[OWN].at[pl.ds(0, FOOT)], local.at[1])
    own_held.start()
    for slot in range(SLOTS):
        held[slot][FOOT] = jnp.zeros((ROWS, WIDTH), BF16)

    kron_rows(sx, wide_x, kx)
    wide = iota((TILES, WIDTH), 1)
    spread = (iota((TILES, WIDTH), 0) == (wide // 128) * TILE + wide % TILE).astype(BF16)
    rows_y = dot(sy[...], spread)
    level = (iota((TILE, WIDTH), 1) // TILE) % 8
    for b in range(4):
        for z in range(8):
            ky[(b * 8 + z) * TILE : (b * 8 + z + 1) * TILE, :] = jnp.where(
                level == z, rows_y[b * TILE : (b + 1) * TILE, :], 0.0
            ).astype(BF16)
    kron_rows(sz, wide_z, wz)

    def smooth_plane(slot, index):
        def along_x(b, carry):
            for x in range(16):
                dense[x * ROWS : (x + 1) * ROWS, :] = held[slot][index(b * 16 + x)]
            mixed = dot(kx[...], dense[...]).astype(BF16)
            for g in range(4):
                across[g, :, pl.ds(pl.multiple_of(b * 128, 128), 128)] = mixed[:, g * 128 : (g + 1) * 128]
            return carry

        lax.fori_loop(0, 4, along_x, 0)

        def along_y(g, carry):
            mixed = dot(across[g], ky[...]).astype(BF16)
            for e in range(4):
                field[
                    e * 16 : (e + 1) * 16, slot * ROWS : (slot + 1) * ROWS, pl.ds(pl.multiple_of(g * 128, 128), 128)
                ] = mixed[:, e * 128 : (e + 1) * 128].reshape(16, ROWS, 128)
            return carry

        lax.fori_loop(0, 4, along_y, 0)

    def take_table(slot):
        copy = pltpu.make_async_copy(tables[slot], inv_smem[slot], local.at[2 + slot])
        copy.start()
        copy.wait()

    own_held.wait()
    smooth_plane(OWN, lambda i: inv_own[0, i])

    def send_second(j, k):
        f0, fn = CHUNKS[k]
        to = lax.rem(c + j, CELLS)
        return remote(
            second.at[to, pl.ds(f0, fn)], smoothed.at[pl.ds(c * PART + f0, fn)],
            z2_send.at[j - 1, k], z2_recv.at[j - 1, k], s, to,
        )

    def recv_second(j, k):
        f0, fn = CHUNKS[k]
        came = lax.rem(c + CELLS - j, CELLS)
        return remote(
            second.at[came, pl.ds(f0, fn)], smoothed.at[pl.ds(came * PART + f0, fn)],
            z2_send.at[j - 1, k], z2_recv.at[j - 1, k], s, came,
        )

    def own_second(k):
        f0, fn = CHUNKS[k]
        return pltpu.make_async_copy(
            second.at[c, pl.ds(f0, fn)], smoothed.at[pl.ds(c * PART + f0, fn)], local.at[7 + k]
        )

    def smooth_depth(k):
        f0, fn = CHUNKS[k]
        for j in (1, 2, 3):
            recv_first(j, k).wait_recv()
        if k == 0:
            own_first.wait()
        rows = jnp.concatenate(
            [first[d, f0 : f0 + fn].reshape(fn * ROWS, WIDTH) for d in range(CELLS)], axis=1
        )
        for j in (2, 1, 3, 0):
            to = lax.rem(c + j, CELLS)
            done = dot(rows, wz[:, pl.ds(pl.multiple_of(to * WIDTH, WIDTH), WIDTH)])
            second[to, f0 : f0 + fn] = done.astype(BF16).reshape(fn, ROWS, WIDTH)
            if j:
                send_second(j, k).start()
            else:
                own_second(k).start()

    @pl.when(hops)
    def _():
        for p in range(PIECES[ASIDE]):
            sent_hop[p].wait_recv()
            past_hop[p].start()

    smooth_depth(0)

    for slot, p, source, relay_at, target in RELAYED:
        @pl.when(place == relay_at)
        def _(slot=slot, p=p, source=source, target=target):
            to_relay(slot, p, h_send.at[BEHIND, 0], beyond + source).wait_recv()
            from_relay(slot, p, here + target).start()

    onward = jnp.logical_and(inner, is_odd)
    for p in range(PIECES[BEHIND]):
        sent_behind[p].wait_recv()

        @pl.when(onward)
        def _(p=p):
            sent_far[p].start()

    begin(sent_beside)
    sent_tables[0].wait_recv()
    take_table(BEHIND)
    smooth_plane(BEHIND, lambda i: inv_smem[BEHIND][0, i])

    for p in range(PIECES[ASIDE]):
        sent_aside[p].wait_recv()

    @pl.when(is_odd)
    def _():
        begin(over_far)

    sent_tables[2].wait_recv()
    take_table(ASIDE)
    smooth_plane(ASIDE, lambda i: inv_smem[ASIDE][0, i])

    smooth_depth(1)

    sent_beside[0].wait_recv()
    sent_tables[1].wait_recv()
    take_table(BESIDE)
    smooth_plane(BESIDE, lambda i: inv_smem[BESIDE][0, i])

    for p in range(PIECES[FAR]):
        sent_far[p].wait_recv()
    sent_tables[3].wait_recv()
    take_table(FAR)
    smooth_plane(FAR, lambda i: inv_smem[FAR][0, i])

    total = jnp.zeros((ROWS, SLOTS * ROWS), F32)
    for k, (f0, fn) in enumerate(CHUNKS):
        own_second(k).wait()
        for j in (1, 2, 3):
            recv_second(j, k).wait_recv()

        def product(e, total, f0=f0, fn=fn):
            for f in range(f0, f0 + fn):
                place = e * PART + f
                total = total + lax.dot_general(
                    smoothed[place], field[foot_own[0, place]],
                    (((1,), (1,)), ((), ())), preferred_element_type=F32,
                )
            return total

        total = lax.fori_loop(0, CELLS, product, total)

    square[...] = jnp.zeros((128, 128), F32)
    square[0:ROWS, 0 : SLOTS * ROWS] = total
    flipped = square[...].T
    back = {}
    for i, slot in enumerate((BEHIND, BESIDE, FAR, ASIDE)):
        turned[i] = flipped[slot * ROWS : (slot + 1) * ROWS, :]
    partners = (at(-2), at(-1 - 2 * odd), at(4 - 8 * odd), at(1 + 2 * odd))
    for i in range(4):
        back[i] = remote(turned.at[i], turned_in.at[i], b_send.at[i], b_recv.at[i], partners[i], c)
        back[i].start()
    for i in range(4):
        back[i].wait_recv()

    def mine(slot):
        return total[:, slot * ROWS : (slot + 1) * ROWS]

    def theirs(i):
        return turned_in[i][:, :ROWS]

    beside, aside, far = mine(BESIDE), mine(ASIDE), mine(FAR)
    parts = [
        jnp.where(is_odd, far, theirs(2)),
        jnp.where(is_odd, beside, theirs(3)),
        mine(BEHIND),
        jnp.where(is_odd, theirs(3), beside),
        mine(OWN),
        jnp.where(is_odd, theirs(1), aside),
        theirs(0),
        jnp.where(is_odd, aside, theirs(1)),
        jnp.where(is_odd, theirs(2), far),
    ]
    whole = jnp.concatenate(parts, axis=1) * link[0:1, 0 : BAND * ROWS]
    for e in range(CELLS):
        shares[e, :, 0:SHARE] = whole[:, e * SHARE : (e + 1) * SHARE]
    given = []
    for j in (1, 2, 3):
        to = lax.rem(c + j, CELLS)
        copy = remote(shares.at[to], shares_in.at[j - 1], c_send.at[j - 1], c_recv.at[j - 1], s, to)
        copy.start()
        given.append(copy)
    for copy in given:
        copy.wait_recv()
    summed = shares[c] + shares_in[0] + shares_in[1] + shares_in[2]
    out[...] = summed[:, 0:SHARE]

    for k in range(len(CHUNKS)):
        for j in (1, 2, 3):
            send_first(j, k).wait_send()
            send_second(j, k).wait_send()
    for copy in (*sent_tables, *sent_behind, *sent_aside, *sent_beside, *back.values(), *given):
        copy.wait_send()

    @pl.when(onward)
    def _():
        for copy in sent_far:
            copy.wait_send()

    @pl.when(is_odd)
    def _():
        for copy in over_far:
            copy.wait_send()

    @pl.when(hops)
    def _():
        for copy in past_hop:
            copy.wait_send()

    @pl.when(place == 61)
    def _():
        for p in range(PIECES[FAR]):
            halo(FAR, p, x_hbm, cross_send.at[p], beyond + 1).wait_send()

    for slot, p, source, relay_at, target in RELAYED:
        @pl.when(place == relay_at)
        def _(slot=slot, p=p, target=target):
            from_relay(slot, p, here + target).wait_send()


def body(sensitivity, footprint, linked, smooth_x, smooth_y, smooth_z):
    values = jnp.transpose(sensitivity, (1, 0, 2))
    tiles = jnp.arange(TILES, dtype=jnp.int32)
    tile_of = (tiles % 16) * 4 + tiles // 16
    match = footprint[0][None, :] == tile_of[:, None]
    order = jnp.arange(FOOT, dtype=jnp.int32)[None, :]
    inverse = FOOT + jnp.sum(jnp.where(match, order - FOOT, 0), axis=1)
    inverse = jnp.broadcast_to(jnp.pad(inverse, (0, 128 - TILES))[None, :], (8, 128))
    foot = (footprint % 4) * 16 + footprint // 4
    link = jnp.repeat(linked.astype(F32), ROWS, axis=1)
    n_k = len(CHUNKS)
    vmem = pl.BlockSpec(memory_space=pltpu.VMEM)
    smem = pl.BlockSpec(memory_space=pltpu.SMEM)
    dma = pltpu.SemaphoreType.DMA
    return pl.pallas_call(
        kernel,
        out_shape=jax.ShapeDtypeStruct((ROWS, SHARE), F32),
        in_specs=[pl.BlockSpec(memory_space=pl.ANY), smem, smem, vmem, vmem, vmem, vmem, vmem],
        out_specs=vmem,
        scratch_shapes=[
            [pltpu.VMEM((FOOT + 1, ROWS, WIDTH), BF16)] * SLOTS,
            [pltpu.VMEM((8, 128), jnp.int32)] * SLOTS,
            [pltpu.SMEM((8, 128), jnp.int32)] * SLOTS,
            pltpu.VMEM((CELLS, PART, ROWS, WIDTH), BF16),
            pltpu.VMEM((CELLS, PART, ROWS, WIDTH), BF16),
            pltpu.VMEM((FOOT, ROWS, WIDTH), BF16),
            pltpu.VMEM((2048, 2048), BF16),
            pltpu.VMEM((256, 256), BF16),
            pltpu.VMEM((512, 512), BF16),
            pltpu.VMEM((128, 2048), F32),
            pltpu.VMEM((16, 256), F32),
            pltpu.VMEM((256, WIDTH), BF16),
            pltpu.VMEM((4, 256, WIDTH), BF16),
            pltpu.VMEM((TILES, SLOTS * ROWS, WIDTH), BF16),
            pltpu.VMEM((128, 128), F32),
            pltpu.VMEM((4, ROWS, 128), F32),
            pltpu.VMEM((4, ROWS, 128), F32),
            pltpu.VMEM((CELLS, ROWS, 128), F32),
            pltpu.VMEM((CELLS - 1, ROWS, 128), F32),
            dma((3, n_k)), dma((3, n_k)), dma((3, n_k)), dma((3, n_k)),
            dma((SLOTS, 4)), dma((SLOTS, 4)), dma((SLOTS,)), dma((SLOTS,)),
            dma((4,)), dma((4,)), dma((3,)), dma((3,)), dma((10,)),
            pltpu.VMEM((FOOT // 2, ROWS, WIDTH), BF16), dma((4,)), dma((1,)), dma((1,)),
            pltpu.VMEM((FOOT, ROWS, WIDTH), BF16), dma((2,)), dma((2,)), dma((4,)),
        ],
        compiler_params=pltpu.CompilerParams(
            collective_id=0, has_side_effects=True, vmem_limit_bytes=56 * 2**20
        ),
        name="band",
    )(values, inverse, foot, inverse, link, smooth_x, smooth_y, smooth_z)


def solution(mesh):
    return jax.shard_map(
        body,
        mesh=mesh,
        in_specs=(P("sta", None, "cell"), P("sta", None), P("sta", None), P(), P(), P()),
        out_specs=P("sta", "cell"),
        check_vma=False,
    )
```

```python
import jax
import jax.numpy as jnp
from jax import lax
from jax.experimental import pallas as pl
from jax.experimental.pallas import tpu as pltpu
from jax.sharding import PartitionSpec as P

TILE = 16
FOOT = 52
TILES = 64
BAND = 9
ROWS = 16
WIDTH = 512
CELLS = 4
STAS = 128
PART = FOOT // CELLS
CHUNKS = ((0, 7), (7, 6))
SHARE = BAND * ROWS // CELLS
MESH = pl.DeviceIdType.MESH
OWN, BEHIND, BESIDE, ASIDE, FAR = range(5)
SLOTS = 5
F32, BF16 = jnp.float32, jnp.bfloat16
PIECES = {BEHIND: 8, BESIDE: 1, ASIDE: 8, FAR: 8}
ROW_STAS = 8
HALF_STAS = 64


CROSSINGS = (
    (BEHIND, 62, 0, 0, 0), (BEHIND, 63, 1, 1, 0), (FAR, 61, 3, 1, 0), (ASIDE, 0, 2, 61, 7), (ASIDE, 2, 4, 63, 7)
)


def relay_rows(direct):
    return [row for row in range(8) if row != direct]


def iota(shape, dim):
    return lax.broadcasted_iota(jnp.int32, shape, dim)


def dot(a, b):
    return jnp.dot(a, b, preferred_element_type=F32)


def kron_rows(small_ref, wide_ref, big_ref):
    n = small_ref.shape[0]
    repeat = (iota((n, n * TILE), 0) == iota((n, n * TILE), 1) // TILE).astype(BF16)
    wide_ref[...] = dot(small_ref[...], repeat)
    same = iota((TILE, n * TILE), 0) == iota((TILE, n * TILE), 1) % TILE

    def row(a, carry):
        line = jnp.broadcast_to(wide_ref[pl.ds(a, 1), :], (TILE, n * TILE))
        big_ref[pl.ds(pl.multiple_of(a * TILE, TILE), TILE), :] = jnp.where(same, line, 0.0).astype(BF16)
        return carry

    lax.fori_loop(0, n, row, 0)


def kernel(
    x_hbm, inv_own, foot_own, inv_vmem, link, sx, sy, sz, out,
    held, tables, inv_smem, first, second, smoothed, wz, kx, ky, wide_z, wide_x,
    dense, across, field, square, turned, turned_in, shares, shares_in,
    z1_send, z1_recv, z2_send, z2_recv, h_send, h_recv, t_send, t_recv,
    b_send, b_recv, c_send, c_recv, local, relay, cross_send, relay_send, relay_recv,
    hop, hop_send, hop_recv, over_send,
):
    s = lax.axis_index("sta")
    c = lax.axis_index("cell")
    odd = lax.rem(s, 2)

    def at(distance):
        return lax.rem(s + distance + STAS, STAS)

    def remote(src, dst, send, recv, sta, cell):
        return pltpu.make_async_remote_copy(
            src_ref=src, dst_ref=dst, send_sem=send, recv_sem=recv,
            device_id=(sta, cell), device_id_type=MESH,
        )

    sibling = s + 1 - 2 * odd
    aside_to = at(-3 + 2 * odd)
    place = lax.rem(s, HALF_STAS)
    here = s - place
    beyond = HALF_STAS - here

    barrier = pltpu.get_barrier_semaphore()
    for distance in (-4, -3, -2, -1, 1, 2, 3, 4):
        pl.semaphore_signal(barrier, inc=1, device_id=(at(distance), c), device_id_type=MESH)
    for j in (1, 2, 3):
        pl.semaphore_signal(barrier, inc=1, device_id=(s, lax.rem(c + j, CELLS)), device_id_type=MESH)
    row, column = place // ROW_STAS, lax.rem(place, ROW_STAS)
    relays = [jnp.logical_and(column == col, row != direct) for _, _, col, _, direct in CROSSINGS]
    greeted = jnp.int32(11)
    for acts, (slot, source, col, target, direct) in zip(relays, CROSSINGS):
        greeted += jnp.where(acts, 1, 0) + jnp.where(place == source, 7, 0)

        @pl.when(acts)
        def _(source=source):
            pl.semaphore_signal(barrier, inc=1, device_id=(beyond + source, c), device_id_type=MESH)

        @pl.when(place == target)
        def _(col=col, direct=direct):
            for r in relay_rows(direct):
                pl.semaphore_signal(barrier, inc=1, device_id=(here + r * ROW_STAS + col, c), device_id_type=MESH)

    pl.semaphore_wait(barrier, greeted)

    def send_first(j, k):
        f0, fn = CHUNKS[k]
        to = lax.rem(c + j, CELLS)
        return remote(
            x_hbm.at[pl.ds(to * PART + f0, fn)], first.at[c, pl.ds(f0, fn)],
            z1_send.at[j - 1, k], z1_recv.at[j - 1, k], s, to,
        )

    def recv_first(j, k):
        f0, fn = CHUNKS[k]
        came = lax.rem(c + CELLS - j, CELLS)
        return remote(
            x_hbm.at[pl.ds(f0, fn)], first.at[came, pl.ds(f0, fn)],
            z1_send.at[j - 1, k], z1_recv.at[j - 1, k], s, came,
        )

    for k in range(len(CHUNKS)):
        for j in (2, 1, 3):
            send_first(j, k).start()

    def size_of(slot, p):
        return FOOT if PIECES[slot] == 1 else 7 if p < 4 else 6

    def cut(slot, p):
        return pl.ds(6 * p + min(p, 4), size_of(slot, p))

    def halo(slot, p, src, send, sta):
        return remote(src.at[cut(slot, p)], held[slot].at[cut(slot, p)], send, h_recv.at[slot, p], sta, c)

    def halos(slot, src, sta):
        return [halo(slot, p, src, h_send.at[slot, p], sta) for p in range(PIECES[slot])]

    def begin(copies):
        for copy in copies:
            copy.start()

    def to_relay(slot, p, send, sta):
        return remote(
            x_hbm.at[cut(slot, p)], relay.at[pl.ds(0, size_of(slot, p))], send, relay_recv.at[0], sta, c
        )

    def from_relay(slot, p, size, start, sta):
        return remote(
            relay.at[pl.ds(0, size)], held[slot].at[pl.ds(start, size)],
            relay_send.at[0], h_recv.at[slot, p], sta, c,
        )

    def relaying(begins):
        for acts, (slot, source, col, target, direct) in zip(relays, CROSSINGS):
            p = row if direct == 0 else row + 1
            for size, fits in ((7, p < 4), (6, p >= 4)):
                @pl.when(jnp.logical_and(acts, fits))
                def _(slot=slot, source=source, target=target, p=p, size=size):
                    start = 6 * p + (0 if size == 7 else 4)
                    if size == 7:
                        start = 7 * p
                    if begins:
                        to_relay(slot, 0 if size == 7 else 4, h_send.at[BEHIND, 0], beyond + source).wait_recv()
                        from_relay(slot, p, size, start, here + target).start()
                    else:
                        from_relay(slot, p, size, start, here + target).wait_send()

    def table(slot, sta):
        return remote(inv_vmem, tables[slot], t_send.at[slot], t_recv.at[slot], sta, c)

    sent_tables = [
        table(BEHIND, at(2)), table(BESIDE, at(3 - 2 * odd)), table(ASIDE, aside_to), table(FAR, at(8 * odd - 4))
    ]
    begin(sent_tables)
    sent_behind = halos(BEHIND, x_hbm, at(2))
    sent_aside = halos(ASIDE, x_hbm, aside_to)
    sent_far = halos(FAR, held[BEHIND], at(2))
    over_far = [halo(FAR, p, held[ASIDE], over_send.at[p], sibling) for p in range(PIECES[FAR])]
    sent_beside = halos(BESIDE, held[BEHIND], sibling)
    inner = place < 62
    is_odd = odd == 1
    hopping = jnp.logical_and(odd == 0, place >= 4)
    hops = jnp.logical_and(odd == 0, jnp.logical_and(place >= 2, place <= 60))
    sent_hop = [
        remote(x_hbm.at[cut(ASIDE, p)], hop.at[cut(ASIDE, p)], h_send.at[ASIDE, p], hop_recv.at[p], at(-2), c)
        for p in range(PIECES[ASIDE])
    ]
    past_hop = [halo(ASIDE, p, hop, hop_send.at[p], at(-1)) for p in range(PIECES[ASIDE])]

    @pl.when(inner)
    def _():
        begin(sent_behind)

    @pl.when(is_odd)
    def _():
        begin(sent_aside)

    @pl.when(hopping)
    def _():
        begin(sent_hop)

    for slot, source, col, target, direct in CROSSINGS:
        @pl.when(place == source)
        def _(slot=slot, col=col, target=target, direct=direct):
            sends = [cross_send.at[p] if slot == FAR else h_send.at[slot, p] for p in range(8)]
            for p, r in enumerate(relay_rows(direct), 1):
                to_relay(slot, p, sends[p], beyond + r * ROW_STAS + col).start()
            halo(slot, 0, x_hbm, sends[0], beyond + target).start()

    own_first = pltpu.make_async_copy(x_hbm.at[pl.ds(c * PART, PART)], first.at[c], local.at[0])
    own_first.start()
    own_held = pltpu.make_async_copy(x_hbm, held[OWN].at[pl.ds(0, FOOT)], local.at[1])
    own_held.start()
    for slot in range(SLOTS):
        held[slot][FOOT] = jnp.zeros((ROWS, WIDTH), BF16)

    kron_rows(sx, wide_x, kx)
    wide = iota((TILES, WIDTH), 1)
    spread = (iota((TILES, WIDTH), 0) == (wide // 128) * TILE + wide % TILE).astype(BF16)
    rows_y = dot(sy[...], spread)
    level = (iota((TILE, WIDTH), 1) // TILE) % 8
    for b in range(4):
        for z in range(8):
            ky[(b * 8 + z) * TILE : (b * 8 + z + 1) * TILE, :] = jnp.where(
                level == z, rows_y[b * TILE : (b + 1) * TILE, :], 0.0
            ).astype(BF16)
    kron_rows(sz, wide_z, wz)

    def smooth_plane(slot, index):
        def along_x(b, carry):
            for x in range(16):
                dense[x * ROWS : (x + 1) * ROWS, :] = held[slot][index(b * 16 + x)]
            mixed = dot(kx[...], dense[...]).astype(BF16)
            for g in range(4):
                across[g, :, pl.ds(pl.multiple_of(b * 128, 128), 128)] = mixed[:, g * 128 : (g + 1) * 128]
            return carry

        lax.fori_loop(0, 4, along_x, 0)

        def along_y(g, carry):
            mixed = dot(across[g], ky[...]).astype(BF16)
            for e in range(4):
                field[
                    e * 16 : (e + 1) * 16, slot * ROWS : (slot + 1) * ROWS, pl.ds(pl.multiple_of(g * 128, 128), 128)
                ] = mixed[:, e * 128 : (e + 1) * 128].reshape(16, ROWS, 128)
            return carry

        lax.fori_loop(0, 4, along_y, 0)

    def take_table(slot):
        copy = pltpu.make_async_copy(tables[slot], inv_smem[slot], local.at[2 + slot])
        copy.start()
        copy.wait()

    own_held.wait()
    smooth_plane(OWN, lambda i: inv_own[0, i])

    def send_second(j, k):
        f0, fn = CHUNKS[k]
        to = lax.rem(c + j, CELLS)
        return remote(
            second.at[to, pl.ds(f0, fn)], smoothed.at[pl.ds(c * PART + f0, fn)],
            z2_send.at[j - 1, k], z2_recv.at[j - 1, k], s, to,
        )

    def recv_second(j, k):
        f0, fn = CHUNKS[k]
        came = lax.rem(c + CELLS - j, CELLS)
        return remote(
            second.at[came, pl.ds(f0, fn)], smoothed.at[pl.ds(came * PART + f0, fn)],
            z2_send.at[j - 1, k], z2_recv.at[j - 1, k], s, came,
        )

    def own_second(k):
        f0, fn = CHUNKS[k]
        return pltpu.make_async_copy(
            second.at[c, pl.ds(f0, fn)], smoothed.at[pl.ds(c * PART + f0, fn)], local.at[7 + k]
        )

    def smooth_depth(k):
        f0, fn = CHUNKS[k]
        for j in (1, 2, 3):
            recv_first(j, k).wait_recv()
        if k == 0:
            own_first.wait()
        rows = jnp.concatenate(
            [first[d, f0 : f0 + fn].reshape(fn * ROWS, WIDTH) for d in range(CELLS)], axis=1
        )
        for j in (2, 1, 3, 0):
            to = lax.rem(c + j, CELLS)
            done = dot(rows, wz[:, pl.ds(pl.multiple_of(to * WIDTH, WIDTH), WIDTH)])
            second[to, f0 : f0 + fn] = done.astype(BF16).reshape(fn, ROWS, WIDTH)
            if j:
                send_second(j, k).start()
            else:
                own_second(k).start()

    @pl.when(hops)
    def _():
        for p in range(PIECES[ASIDE]):
            sent_hop[p].wait_recv()
            past_hop[p].start()

    relaying(True)

    smooth_depth(0)

    onward = jnp.logical_and(inner, is_odd)
    for p in range(PIECES[BEHIND]):
        sent_behind[p].wait_recv()

        @pl.when(onward)
        def _(p=p):
            sent_far[p].start()

    begin(sent_beside)
    sent_tables[0].wait_recv()
    take_table(BEHIND)
    smooth_plane(BEHIND, lambda i: inv_smem[BEHIND][0, i])

    for p in range(PIECES[ASIDE]):
        sent_aside[p].wait_recv()

    @pl.when(is_odd)
    def _():
        begin(over_far)

    sent_tables[2].wait_recv()
    take_table(ASIDE)
    smooth_plane(ASIDE, lambda i: inv_smem[ASIDE][0, i])

    smooth_depth(1)

    sent_beside[0].wait_recv()
    sent_tables[1].wait_recv()
    take_table(BESIDE)
    smooth_plane(BESIDE, lambda i: inv_smem[BESIDE][0, i])

    for p in range(PIECES[FAR]):
        sent_far[p].wait_recv()
    sent_tables[3].wait_recv()
    take_table(FAR)
    smooth_plane(FAR, lambda i: inv_smem[FAR][0, i])

    total = jnp.zeros((ROWS, SLOTS * ROWS), F32)
    for k, (f0, fn) in enumerate(CHUNKS):
        own_second(k).wait()
        for j in (1, 2, 3):
            recv_second(j, k).wait_recv()

        def product(e, total, f0=f0, fn=fn):
            for f in range(f0, f0 + fn):
                place = e * PART + f
                total = total + lax.dot_general(
                    smoothed[place], field[foot_own[0, place]],
                    (((1,), (1,)), ((), ())), preferred_element_type=F32,
                )
            return total

        total = lax.fori_loop(0, CELLS, product, total)

    square[...] = jnp.zeros((128, 128), F32)
    square[0:ROWS, 0 : SLOTS * ROWS] = total
    flipped = square[...].T
    back = {}
    for i, slot in enumerate((BEHIND, BESIDE, FAR, ASIDE)):
        turned[i] = flipped[slot * ROWS : (slot + 1) * ROWS, :]
    partners = (at(-2), at(-1 - 2 * odd), at(4 - 8 * odd), at(1 + 2 * odd))
    for i in range(4):
        back[i] = remote(turned.at[i], turned_in.at[i], b_send.at[i], b_recv.at[i], partners[i], c)
        back[i].start()
    for i in range(4):
        back[i].wait_recv()

    def mine(slot):
        return total[:, slot * ROWS : (slot + 1) * ROWS]

    def theirs(i):
        return turned_in[i][:, :ROWS]

    beside, aside, far = mine(BESIDE), mine(ASIDE), mine(FAR)
    parts = [
        jnp.where(is_odd, far, theirs(2)),
        jnp.where(is_odd, beside, theirs(3)),
        mine(BEHIND),
        jnp.where(is_odd, theirs(3), beside),
        mine(OWN),
        jnp.where(is_odd, theirs(1), aside),
        theirs(0),
        jnp.where(is_odd, aside, theirs(1)),
        jnp.where(is_odd, theirs(2), far),
    ]
    whole = jnp.concatenate(parts, axis=1) * link[0:1, 0 : BAND * ROWS]
    for e in range(CELLS):
        shares[e, :, 0:SHARE] = whole[:, e * SHARE : (e + 1) * SHARE]
    given = []
    for j in (1, 2, 3):
        to = lax.rem(c + j, CELLS)
        copy = remote(shares.at[to], shares_in.at[j - 1], c_send.at[j - 1], c_recv.at[j - 1], s, to)
        copy.start()
        given.append(copy)
    for copy in given:
        copy.wait_recv()
    summed = shares[c] + shares_in[0] + shares_in[1] + shares_in[2]
    out[...] = summed[:, 0:SHARE]

    for k in range(len(CHUNKS)):
        for j in (1, 2, 3):
            send_first(j, k).wait_send()
            send_second(j, k).wait_send()
    for copy in (*sent_tables, *sent_behind, *sent_aside, *sent_beside, *back.values(), *given):
        copy.wait_send()

    @pl.when(onward)
    def _():
        for copy in sent_far:
            copy.wait_send()

    @pl.when(is_odd)
    def _():
        for copy in over_far:
            copy.wait_send()

    @pl.when(hops)
    def _():
        for copy in past_hop:
            copy.wait_send()

    @pl.when(place == 61)
    def _():
        for p in range(PIECES[FAR]):
            halo(FAR, p, x_hbm, cross_send.at[p], beyond + 1).wait_send()

    relaying(False)


def body(sensitivity, footprint, linked, smooth_x, smooth_y, smooth_z):
    values = jnp.transpose(sensitivity, (1, 0, 2))
    tiles = jnp.arange(TILES, dtype=jnp.int32)
    tile_of = (tiles % 16) * 4 + tiles // 16
    match = footprint[0][None, :] == tile_of[:, None]
    order = jnp.arange(FOOT, dtype=jnp.int32)[None, :]
    inverse = FOOT + jnp.sum(jnp.where(match, order - FOOT, 0), axis=1)
    inverse = jnp.broadcast_to(jnp.pad(inverse, (0, 128 - TILES))[None, :], (8, 128))
    foot = (footprint % 4) * 16 + footprint // 4
    link = jnp.repeat(linked.astype(F32), ROWS, axis=1)
    n_k = len(CHUNKS)
    vmem = pl.BlockSpec(memory_space=pltpu.VMEM)
    smem = pl.BlockSpec(memory_space=pltpu.SMEM)
    dma = pltpu.SemaphoreType.DMA
    return pl.pallas_call(
        kernel,
        out_shape=jax.ShapeDtypeStruct((ROWS, SHARE), F32),
        in_specs=[pl.BlockSpec(memory_space=pl.ANY), smem, smem, vmem, vmem, vmem, vmem, vmem],
        out_specs=vmem,
        scratch_shapes=[
            [pltpu.VMEM((FOOT + 1, ROWS, WIDTH), BF16)] * SLOTS,
            [pltpu.VMEM((8, 128), jnp.int32)] * SLOTS,
            [pltpu.SMEM((8, 128), jnp.int32)] * SLOTS,
            pltpu.VMEM((CELLS, PART, ROWS, WIDTH), BF16),
            pltpu.VMEM((CELLS, PART, ROWS, WIDTH), BF16),
            pltpu.VMEM((FOOT, ROWS, WIDTH), BF16),
            pltpu.VMEM((2048, 2048), BF16),
            pltpu.VMEM((256, 256), BF16),
            pltpu.VMEM((512, 512), BF16),
            pltpu.VMEM((128, 2048), F32),
            pltpu.VMEM((16, 256), F32),
            pltpu.VMEM((256, WIDTH), BF16),
            pltpu.VMEM((4, 256, WIDTH), BF16),
            pltpu.VMEM((TILES, SLOTS * ROWS, WIDTH), BF16),
            pltpu.VMEM((128, 128), F32),
            pltpu.VMEM((4, ROWS, 128), F32),
            pltpu.VMEM((4, ROWS, 128), F32),
            pltpu.VMEM((CELLS, ROWS, 128), F32),
            pltpu.VMEM((CELLS - 1, ROWS, 128), F32),
            dma((3, n_k)), dma((3, n_k)), dma((3, n_k)), dma((3, n_k)),
            dma((SLOTS, 8)), dma((SLOTS, 8)), dma((SLOTS,)), dma((SLOTS,)),
            dma((4,)), dma((4,)), dma((3,)), dma((3,)), dma((10,)),
            pltpu.VMEM((7, ROWS, WIDTH), BF16), dma((8,)), dma((1,)), dma((1,)),
            pltpu.VMEM((FOOT, ROWS, WIDTH), BF16), dma((8,)), dma((8,)), dma((8,)),
        ],
        compiler_params=pltpu.CompilerParams(
            collective_id=0, has_side_effects=True, vmem_limit_bytes=56 * 2**20
        ),
        name="band",
    )(values, inverse, foot, inverse, link, smooth_x, smooth_y, smooth_z)


def solution(mesh):
    return jax.shard_map(
        body,
        mesh=mesh,
        in_specs=(P("sta", None, "cell"), P("sta", None), P("sta", None), P(), P(), P()),
        out_specs=P("sta", "cell"),
        check_vma=False,
    )
```

```python
import jax
import jax.numpy as jnp
from jax import lax
from jax.experimental import pallas as pl
from jax.experimental.pallas import tpu as pltpu
from jax.sharding import PartitionSpec as P

TILE = 16
FOOT = 52
TILES = 64
BAND = 9
ROWS = 16
WIDTH = 512
CELLS = 4
STAS = 128
PART = FOOT // CELLS
CHUNKS = ((0, 7), (7, 6))
SHARE = BAND * ROWS // CELLS
MESH = pl.DeviceIdType.MESH
OWN, BEHIND, BESIDE, ASIDE, FAR = range(5)
SLOTS = 5
F32, BF16 = jnp.float32, jnp.bfloat16
PIECES = {BEHIND: 8, BESIDE: 1, ASIDE: 8, FAR: 8}
ROW_STAS = 8
HALF_STAS = 64


CROSSINGS = (
    (BEHIND, 62, 0, 0, 0), (BEHIND, 63, 1, 1, 0), (FAR, 61, 3, 1, 0), (ASIDE, 0, 2, 61, 7), (ASIDE, 2, 4, 63, 7)
)


def relay_rows(direct):
    return [row for row in range(8) if row != direct]


def iota(shape, dim):
    return lax.broadcasted_iota(jnp.int32, shape, dim)


def dot(a, b):
    return jnp.dot(a, b, preferred_element_type=F32)


def kron_rows(small_ref, wide_ref, big_ref):
    n = small_ref.shape[0]
    repeat = (iota((n, n * TILE), 0) == iota((n, n * TILE), 1) // TILE).astype(BF16)
    wide_ref[...] = dot(small_ref[...], repeat)
    same = iota((TILE, n * TILE), 0) == iota((TILE, n * TILE), 1) % TILE

    def row(a, carry):
        line = jnp.broadcast_to(wide_ref[pl.ds(a, 1), :], (TILE, n * TILE))
        big_ref[pl.ds(pl.multiple_of(a * TILE, TILE), TILE), :] = jnp.where(same, line, 0.0).astype(BF16)
        return carry

    lax.fori_loop(0, n, row, 0)


def kernel(
    x_hbm, foot_own, linked, sx_hbm, sy_hbm, sz_hbm, out,
    inv_own, inv_vmem, sx, sy, sz, held, tables, inv_smem, first, second, smoothed, wz, kx, ky, wide_z, wide_x,
    dense, across, field, square, turned, turned_in, shares, shares_in,
    z1_send, z1_recv, z2_send, z2_recv, h_send, h_recv, t_send, t_recv,
    b_send, b_recv, c_send, c_recv, local, relay, cross_send, relay_send, relay_recv,
    hop, hop_send, hop_recv, over_send,
):
    s = lax.axis_index("sta")
    c = lax.axis_index("cell")
    odd = lax.rem(s, 2)

    def at(distance):
        return lax.rem(s + distance + STAS, STAS)

    def remote(src, dst, send, recv, sta, cell):
        return pltpu.make_async_remote_copy(
            src_ref=src, dst_ref=dst, send_sem=send, recv_sem=recv,
            device_id=(sta, cell), device_id_type=MESH,
        )

    sibling = s + 1 - 2 * odd
    aside_to = at(-3 + 2 * odd)
    place = lax.rem(s, HALF_STAS)
    here = s - place
    beyond = HALF_STAS - here

    fetched = [
        pltpu.make_async_copy(src, dst, local.at[9 + i])
        for i, (src, dst) in enumerate(((sx_hbm, sx), (sy_hbm, sy), (sz_hbm, sz)))
    ]
    for copy in fetched:
        copy.start()
    barrier = pltpu.get_barrier_semaphore()
    for distance in (-4, -3, -2, -1, 1, 2, 3, 4):
        pl.semaphore_signal(barrier, inc=1, device_id=(at(distance), c), device_id_type=MESH)
    for j in (1, 2, 3):
        pl.semaphore_signal(barrier, inc=1, device_id=(s, lax.rem(c + j, CELLS)), device_id_type=MESH)
    row, column = place // ROW_STAS, lax.rem(place, ROW_STAS)
    relays = [jnp.logical_and(column == col, row != direct) for _, _, col, _, direct in CROSSINGS]
    greeted = jnp.int32(11)
    for acts, (slot, source, col, target, direct) in zip(relays, CROSSINGS):
        greeted += jnp.where(acts, 1, 0) + jnp.where(place == source, 7, 0)

        @pl.when(acts)
        def _(source=source):
            pl.semaphore_signal(barrier, inc=1, device_id=(beyond + source, c), device_id_type=MESH)

        @pl.when(place == target)
        def _(col=col, direct=direct):
            for r in relay_rows(direct):
                pl.semaphore_signal(barrier, inc=1, device_id=(here + r * ROW_STAS + col, c), device_id_type=MESH)

    lanes = iota((8, 128), 1)
    tile_at = lax.rem(lanes, 16) * 4 + lanes // 16
    inverse = jnp.full((8, 128), FOOT, jnp.int32)
    for f in range(FOOT):
        inverse = jnp.where(tile_at == foot_own[0, f], f, inverse)
    inv_vmem[...] = inverse

    pl.semaphore_wait(barrier, greeted)

    def send_first(j, k):
        f0, fn = CHUNKS[k]
        to = lax.rem(c + j, CELLS)
        return remote(
            x_hbm.at[pl.ds(to * PART + f0, fn)], first.at[c, pl.ds(f0, fn)],
            z1_send.at[j - 1, k], z1_recv.at[j - 1, k], s, to,
        )

    def recv_first(j, k):
        f0, fn = CHUNKS[k]
        came = lax.rem(c + CELLS - j, CELLS)
        return remote(
            x_hbm.at[pl.ds(f0, fn)], first.at[came, pl.ds(f0, fn)],
            z1_send.at[j - 1, k], z1_recv.at[j - 1, k], s, came,
        )

    for k in range(len(CHUNKS)):
        for j in (2, 1, 3):
            send_first(j, k).start()

    def size_of(slot, p):
        return FOOT if PIECES[slot] == 1 else 7 if p < 4 else 6

    def cut(slot, p):
        return pl.ds(6 * p + min(p, 4), size_of(slot, p))

    def halo(slot, p, src, send, sta):
        return remote(src.at[cut(slot, p)], held[slot].at[cut(slot, p)], send, h_recv.at[slot, p], sta, c)

    def halos(slot, src, sta):
        return [halo(slot, p, src, h_send.at[slot, p], sta) for p in range(PIECES[slot])]

    def begin(copies):
        for copy in copies:
            copy.start()

    def to_relay(slot, p, send, sta):
        return remote(
            x_hbm.at[cut(slot, p)], relay.at[pl.ds(0, size_of(slot, p))], send, relay_recv.at[0], sta, c
        )

    def from_relay(slot, p, size, start, sta):
        return remote(
            relay.at[pl.ds(0, size)], held[slot].at[pl.ds(start, size)],
            relay_send.at[0], h_recv.at[slot, p], sta, c,
        )

    def relaying(begins):
        for acts, (slot, source, col, target, direct) in zip(relays, CROSSINGS):
            p = row if direct == 0 else row + 1
            for size, fits in ((7, p < 4), (6, p >= 4)):
                @pl.when(jnp.logical_and(acts, fits))
                def _(slot=slot, source=source, target=target, p=p, size=size):
                    start = 6 * p + (0 if size == 7 else 4)
                    if size == 7:
                        start = 7 * p
                    if begins:
                        to_relay(slot, 0 if size == 7 else 4, h_send.at[BEHIND, 0], beyond + source).wait_recv()
                        from_relay(slot, p, size, start, here + target).start()
                    else:
                        from_relay(slot, p, size, start, here + target).wait_send()

    def table(slot, sta):
        return remote(inv_vmem, tables[slot], t_send.at[slot], t_recv.at[slot], sta, c)

    sent_tables = [
        table(BEHIND, at(2)), table(BESIDE, at(3 - 2 * odd)), table(ASIDE, aside_to), table(FAR, at(8 * odd - 4))
    ]
    begin(sent_tables)
    sent_behind = halos(BEHIND, x_hbm, at(2))
    sent_aside = halos(ASIDE, x_hbm, aside_to)
    sent_far = halos(FAR, held[BEHIND], at(2))
    over_far = [halo(FAR, p, held[ASIDE], over_send.at[p], sibling) for p in range(PIECES[FAR])]
    sent_beside = halos(BESIDE, held[BEHIND], sibling)
    inner = place < 62
    is_odd = odd == 1
    hopping = jnp.logical_and(odd == 0, place >= 4)
    hops = jnp.logical_and(odd == 0, jnp.logical_and(place >= 2, place <= 60))
    sent_hop = [
        remote(x_hbm.at[cut(ASIDE, p)], hop.at[cut(ASIDE, p)], h_send.at[ASIDE, p], hop_recv.at[p], at(-2), c)
        for p in range(PIECES[ASIDE])
    ]
    past_hop = [halo(ASIDE, p, hop, hop_send.at[p], at(-1)) for p in range(PIECES[ASIDE])]

    @pl.when(inner)
    def _():
        begin(sent_behind)

    @pl.when(is_odd)
    def _():
        begin(sent_aside)

    @pl.when(hopping)
    def _():
        begin(sent_hop)

    for slot, source, col, target, direct in CROSSINGS:
        @pl.when(place == source)
        def _(slot=slot, col=col, target=target, direct=direct):
            sends = [cross_send.at[p] if slot == FAR else h_send.at[slot, p] for p in range(8)]
            for p, r in enumerate(relay_rows(direct), 1):
                to_relay(slot, p, sends[p], beyond + r * ROW_STAS + col).start()
            halo(slot, 0, x_hbm, sends[0], beyond + target).start()

    own_first = pltpu.make_async_copy(x_hbm.at[pl.ds(c * PART, PART)], first.at[c], local.at[0])
    own_first.start()
    own_table = pltpu.make_async_copy(inv_vmem, inv_own, local.at[12])
    own_table.start()
    own_held = pltpu.make_async_copy(x_hbm, held[OWN].at[pl.ds(0, FOOT)], local.at[1])
    own_held.start()
    for slot in range(SLOTS):
        held[slot][FOOT] = jnp.zeros((ROWS, WIDTH), BF16)

    for copy in fetched:
        copy.wait()
    kron_rows(sx, wide_x, kx)
    wide = iota((TILES, WIDTH), 1)
    spread = (iota((TILES, WIDTH), 0) == (wide // 128) * TILE + wide % TILE).astype(BF16)
    rows_y = dot(sy[...], spread)
    level = (iota((TILE, WIDTH), 1) // TILE) % 8
    for b in range(4):
        for z in range(8):
            ky[(b * 8 + z) * TILE : (b * 8 + z + 1) * TILE, :] = jnp.where(
                level == z, rows_y[b * TILE : (b + 1) * TILE, :], 0.0
            ).astype(BF16)
    kron_rows(sz, wide_z, wz)

    def smooth_plane(slot, index):
        def along_x(b, carry):
            for x in range(16):
                dense[x * ROWS : (x + 1) * ROWS, :] = held[slot][index(b * 16 + x)]
            mixed = dot(kx[...], dense[...]).astype(BF16)
            for g in range(4):
                across[g, :, pl.ds(pl.multiple_of(b * 128, 128), 128)] = mixed[:, g * 128 : (g + 1) * 128]
            return carry

        lax.fori_loop(0, 4, along_x, 0)

        def along_y(g, carry):
            mixed = dot(across[g], ky[...]).astype(BF16)
            for e in range(4):
                field[
                    e * 16 : (e + 1) * 16, slot * ROWS : (slot + 1) * ROWS, pl.ds(pl.multiple_of(g * 128, 128), 128)
                ] = mixed[:, e * 128 : (e + 1) * 128].reshape(16, ROWS, 128)
            return carry

        lax.fori_loop(0, 4, along_y, 0)

    def take_table(slot):
        copy = pltpu.make_async_copy(tables[slot], inv_smem[slot], local.at[2 + slot])
        copy.start()
        copy.wait()

    own_held.wait()
    own_table.wait()
    smooth_plane(OWN, lambda i: inv_own[0, i])

    def send_second(j, k):
        f0, fn = CHUNKS[k]
        to = lax.rem(c + j, CELLS)
        return remote(
            second.at[to, pl.ds(f0, fn)], smoothed.at[pl.ds(c * PART + f0, fn)],
            z2_send.at[j - 1, k], z2_recv.at[j - 1, k], s, to,
        )

    def recv_second(j, k):
        f0, fn = CHUNKS[k]
        came = lax.rem(c + CELLS - j, CELLS)
        return remote(
            second.at[came, pl.ds(f0, fn)], smoothed.at[pl.ds(came * PART + f0, fn)],
            z2_send.at[j - 1, k], z2_recv.at[j - 1, k], s, came,
        )

    def own_second(k):
        f0, fn = CHUNKS[k]
        return pltpu.make_async_copy(
            second.at[c, pl.ds(f0, fn)], smoothed.at[pl.ds(c * PART + f0, fn)], local.at[7 + k]
        )

    def smooth_depth(k):
        f0, fn = CHUNKS[k]
        for j in (1, 2, 3):
            recv_first(j, k).wait_recv()
        if k == 0:
            own_first.wait()
        rows = jnp.concatenate(
            [first[d, f0 : f0 + fn].reshape(fn * ROWS, WIDTH) for d in range(CELLS)], axis=1
        )
        for j in (2, 1, 3, 0):
            to = lax.rem(c + j, CELLS)
            done = dot(rows, wz[:, pl.ds(pl.multiple_of(to * WIDTH, WIDTH), WIDTH)])
            second[to, f0 : f0 + fn] = done.astype(BF16).reshape(fn, ROWS, WIDTH)
            if j:
                send_second(j, k).start()
            else:
                own_second(k).start()

    @pl.when(hops)
    def _():
        for p in range(PIECES[ASIDE]):
            sent_hop[p].wait_recv()
            past_hop[p].start()

    relaying(True)

    smooth_depth(0)

    onward = jnp.logical_and(inner, is_odd)
    for p in range(PIECES[BEHIND]):
        sent_behind[p].wait_recv()

        @pl.when(onward)
        def _(p=p):
            sent_far[p].start()

    begin(sent_beside)
    sent_tables[0].wait_recv()
    take_table(BEHIND)
    smooth_plane(BEHIND, lambda i: inv_smem[BEHIND][0, i])

    for p in range(PIECES[ASIDE]):
        sent_aside[p].wait_recv()

    @pl.when(is_odd)
    def _():
        begin(over_far)

    sent_tables[2].wait_recv()
    take_table(ASIDE)
    smooth_plane(ASIDE, lambda i: inv_smem[ASIDE][0, i])

    smooth_depth(1)

    sent_beside[0].wait_recv()
    sent_tables[1].wait_recv()
    take_table(BESIDE)
    smooth_plane(BESIDE, lambda i: inv_smem[BESIDE][0, i])

    for p in range(PIECES[FAR]):
        sent_far[p].wait_recv()
    sent_tables[3].wait_recv()
    take_table(FAR)
    smooth_plane(FAR, lambda i: inv_smem[FAR][0, i])

    total = jnp.zeros((ROWS, SLOTS * ROWS), F32)
    for k, (f0, fn) in enumerate(CHUNKS):
        own_second(k).wait()
        for j in (1, 2, 3):
            recv_second(j, k).wait_recv()

        def product(e, total, f0=f0, fn=fn):
            for f in range(f0, f0 + fn):
                place = e * PART + f
                total = total + lax.dot_general(
                    smoothed[place], field[lax.rem(foot_own[0, place], 4) * 16 + foot_own[0, place] // 4],
                    (((1,), (1,)), ((), ())), preferred_element_type=F32,
                )
            return total

        total = lax.fori_loop(0, CELLS, product, total)

    square[...] = jnp.zeros((128, 128), F32)
    square[0:ROWS, 0 : SLOTS * ROWS] = total
    flipped = square[...].T
    back = {}
    for i, slot in enumerate((BEHIND, BESIDE, FAR, ASIDE)):
        turned[i] = flipped[slot * ROWS : (slot + 1) * ROWS, :]
    partners = (at(-2), at(-1 - 2 * odd), at(4 - 8 * odd), at(1 + 2 * odd))
    for i in range(4):
        back[i] = remote(turned.at[i], turned_in.at[i], b_send.at[i], b_recv.at[i], partners[i], c)
        back[i].start()
    for i in range(4):
        back[i].wait_recv()

    def mine(slot):
        return total[:, slot * ROWS : (slot + 1) * ROWS]

    def theirs(i):
        return turned_in[i][:, :ROWS]

    beside, aside, far = mine(BESIDE), mine(ASIDE), mine(FAR)
    parts = [
        jnp.where(is_odd, far, theirs(2)),
        jnp.where(is_odd, beside, theirs(3)),
        mine(BEHIND),
        jnp.where(is_odd, theirs(3), beside),
        mine(OWN),
        jnp.where(is_odd, theirs(1), aside),
        theirs(0),
        jnp.where(is_odd, aside, theirs(1)),
        jnp.where(is_odd, theirs(2), far),
    ]
    whole = jnp.concatenate([part * linked[0, j].astype(F32) for j, part in enumerate(parts)], axis=1)
    for e in range(CELLS):
        shares[e, :, 0:SHARE] = whole[:, e * SHARE : (e + 1) * SHARE]
    given = []
    for j in (1, 2, 3):
        to = lax.rem(c + j, CELLS)
        copy = remote(shares.at[to], shares_in.at[j - 1], c_send.at[j - 1], c_recv.at[j - 1], s, to)
        copy.start()
        given.append(copy)
    for copy in given:
        copy.wait_recv()
    out[0] = shares[c] + shares_in[0]
    out[1] = shares_in[1] + shares_in[2]

    for k in range(len(CHUNKS)):
        for j in (1, 2, 3):
            send_first(j, k).wait_send()
            send_second(j, k).wait_send()
    for copy in (*sent_tables, *sent_behind, *sent_aside, *sent_beside, *back.values(), *given):
        copy.wait_send()

    @pl.when(onward)
    def _():
        for copy in sent_far:
            copy.wait_send()

    @pl.when(is_odd)
    def _():
        for copy in over_far:
            copy.wait_send()

    @pl.when(hops)
    def _():
        for copy in past_hop:
            copy.wait_send()

    @pl.when(place == 61)
    def _():
        for p in range(PIECES[FAR]):
            halo(FAR, p, x_hbm, cross_send.at[p], beyond + 1).wait_send()

    relaying(False)


def body(sensitivity, footprint, linked, smooth_x, smooth_y, smooth_z):
    values = jnp.transpose(sensitivity, (1, 0, 2))
    n_k = len(CHUNKS)
    vmem = pl.BlockSpec(memory_space=pltpu.VMEM)
    smem = pl.BlockSpec(memory_space=pltpu.SMEM)
    dma = pltpu.SemaphoreType.DMA
    hbm = pl.BlockSpec(memory_space=pl.ANY)
    shared = pl.pallas_call(
        kernel,
        out_shape=jax.ShapeDtypeStruct((2, ROWS, 128), F32),
        in_specs=[hbm, smem, smem, hbm, hbm, hbm],
        out_specs=vmem,
        scratch_shapes=[
            pltpu.SMEM((8, 128), jnp.int32), pltpu.VMEM((8, 128), jnp.int32),
            pltpu.VMEM((16, 16), BF16), pltpu.VMEM((64, 64), BF16), pltpu.VMEM((128, 128), BF16),
            [pltpu.VMEM((FOOT + 1, ROWS, WIDTH), BF16)] * SLOTS,
            [pltpu.VMEM((8, 128), jnp.int32)] * SLOTS,
            [pltpu.SMEM((8, 128), jnp.int32)] * SLOTS,
            pltpu.VMEM((CELLS, PART, ROWS, WIDTH), BF16),
            pltpu.VMEM((CELLS, PART, ROWS, WIDTH), BF16),
            pltpu.VMEM((FOOT, ROWS, WIDTH), BF16),
            pltpu.VMEM((2048, 2048), BF16),
            pltpu.VMEM((256, 256), BF16),
            pltpu.VMEM((512, 512), BF16),
            pltpu.VMEM((128, 2048), F32),
            pltpu.VMEM((16, 256), F32),
            pltpu.VMEM((256, WIDTH), BF16),
            pltpu.VMEM((4, 256, WIDTH), BF16),
            pltpu.VMEM((TILES, SLOTS * ROWS, WIDTH), BF16),
            pltpu.VMEM((128, 128), F32),
            pltpu.VMEM((4, ROWS, 128), F32),
            pltpu.VMEM((4, ROWS, 128), F32),
            pltpu.VMEM((CELLS, ROWS, 128), F32),
            pltpu.VMEM((CELLS - 1, ROWS, 128), F32),
            dma((3, n_k)), dma((3, n_k)), dma((3, n_k)), dma((3, n_k)),
            dma((SLOTS, 8)), dma((SLOTS, 8)), dma((SLOTS,)), dma((SLOTS,)),
            dma((4,)), dma((4,)), dma((3,)), dma((3,)), dma((13,)),
            pltpu.VMEM((7, ROWS, WIDTH), BF16), dma((8,)), dma((1,)), dma((1,)),
            pltpu.VMEM((FOOT, ROWS, WIDTH), BF16), dma((8,)), dma((8,)), dma((8,)),
        ],
        compiler_params=pltpu.CompilerParams(
            collective_id=0, has_side_effects=True, vmem_limit_bytes=56 * 2**20
        ),
        name="band",
    )(values, footprint, linked, smooth_x, smooth_y, smooth_z)
    return (shared[0] + shared[1])[:, :SHARE]


def solution(mesh):
    return jax.shard_map(
        body,
        mesh=mesh,
        in_specs=(P("sta", None, "cell"), P("sta", None), P("sta", None), P(), P(), P()),
        out_specs=P("sta", "cell"),
        check_vma=False,
    )
```

```python
import jax
import jax.numpy as jnp
from jax import lax
from jax.experimental import pallas as pl
from jax.experimental.pallas import tpu as pltpu
from jax.sharding import PartitionSpec as P

TILE = 16
FOOT = 52
TILES = 64
BAND = 9
ROWS = 16
WIDTH = 512
CELLS = 4
STAS = 128
PART = FOOT // CELLS
CHUNKS = ((0, 7), (7, 6))
SHARE = BAND * ROWS // CELLS
MESH = pl.DeviceIdType.MESH
OWN, BEHIND, BESIDE, ASIDE, FAR = range(5)
SLOTS = 5
F32, BF16 = jnp.float32, jnp.bfloat16
PIECES = {BEHIND: 8, BESIDE: 1, ASIDE: 8, FAR: 8}
ROW_STAS = 8
HALF_STAS = 64


CROSSINGS = (
    (BEHIND, 62, 0, 0, 0), (BEHIND, 63, 1, 1, 0), (FAR, 61, 3, 1, 0), (ASIDE, 0, 4, 61, 7), (ASIDE, 2, 6, 63, 7)
)


def relay_rows(direct):
    return [row for row in range(8) if row != direct]


def iota(shape, dim):
    return lax.broadcasted_iota(jnp.int32, shape, dim)


def dot(a, b):
    return jnp.dot(a, b, preferred_element_type=F32)


def kron_rows(small_ref, wide_ref, big_ref):
    n = small_ref.shape[0]
    repeat = (iota((n, n * TILE), 0) == iota((n, n * TILE), 1) // TILE).astype(BF16)
    wide_ref[...] = dot(small_ref[...], repeat)
    same = iota((TILE, n * TILE), 0) == iota((TILE, n * TILE), 1) % TILE

    def row(a, carry):
        line = jnp.broadcast_to(wide_ref[pl.ds(a, 1), :], (TILE, n * TILE))
        big_ref[pl.ds(pl.multiple_of(a * TILE, TILE), TILE), :] = jnp.where(same, line, 0.0).astype(BF16)
        return carry

    lax.fori_loop(0, n, row, 0)


def kernel(
    x_hbm, foot_own, linked, sx_hbm, sy_hbm, sz_hbm, out,
    inv_own, inv_vmem, sx, sy, sz, held, tables, inv_smem, first, second, smoothed, wz, kx, ky, wide_z, wide_x,
    dense, across, field, square, turned, turned_in, shares, shares_in,
    z1_send, z1_recv, z2_send, z2_recv, h_send, h_recv, t_send, t_recv,
    b_send, b_recv, c_send, c_recv, local, relay, cross_send, relay_send, relay_recv,
    hop, hop_send, hop_recv, over_send,
):
    s = lax.axis_index("sta")
    c = lax.axis_index("cell")
    odd = lax.rem(s, 2)

    def at(distance):
        return lax.rem(s + distance + STAS, STAS)

    def remote(src, dst, send, recv, sta, cell):
        return pltpu.make_async_remote_copy(
            src_ref=src, dst_ref=dst, send_sem=send, recv_sem=recv,
            device_id=(sta, cell), device_id_type=MESH,
        )

    sibling = s + 1 - 2 * odd
    aside_to = at(-3 + 2 * odd)
    place = lax.rem(s, HALF_STAS)
    here = s - place
    beyond = HALF_STAS - here

    fetched = [
        pltpu.make_async_copy(src, dst, local.at[9 + i])
        for i, (src, dst) in enumerate(((sx_hbm, sx), (sy_hbm, sy), (sz_hbm, sz)))
    ]
    for copy in fetched:
        copy.start()
    barrier = pltpu.get_barrier_semaphore()
    for distance in (-4, -3, -2, -1, 1, 2, 3, 4):
        pl.semaphore_signal(barrier, inc=1, device_id=(at(distance), c), device_id_type=MESH)
    for j in (1, 2, 3):
        pl.semaphore_signal(barrier, inc=1, device_id=(s, lax.rem(c + j, CELLS)), device_id_type=MESH)
    row, column = place // ROW_STAS, lax.rem(place, ROW_STAS)
    relays = [jnp.logical_and(column == col, row != direct) for _, _, col, _, direct in CROSSINGS]
    greeted = jnp.int32(11)
    for acts, (slot, source, col, target, direct) in zip(relays, CROSSINGS):
        greeted += jnp.where(acts, 1, 0) + jnp.where(place == source, 7, 0)

        @pl.when(acts)
        def _(source=source):
            pl.semaphore_signal(barrier, inc=1, device_id=(beyond + source, c), device_id_type=MESH)

        @pl.when(place == target)
        def _(col=col, direct=direct):
            for r in relay_rows(direct):
                pl.semaphore_signal(barrier, inc=1, device_id=(here + r * ROW_STAS + col, c), device_id_type=MESH)

    lanes = iota((8, 128), 1)
    tile_at = lax.rem(lanes, 16) * 4 + lanes // 16
    inverse = jnp.full((8, 128), FOOT, jnp.int32)
    for f in range(FOOT):
        inverse = jnp.where(tile_at == foot_own[0, f], f, inverse)
    inv_vmem[...] = inverse

    pl.semaphore_wait(barrier, greeted)

    def send_first(j, k):
        f0, fn = CHUNKS[k]
        to = lax.rem(c + j, CELLS)
        return remote(
            x_hbm.at[pl.ds(to * PART + f0, fn)], first.at[c, pl.ds(f0, fn)],
            z1_send.at[j - 1, k], z1_recv.at[j - 1, k], s, to,
        )

    def recv_first(j, k):
        f0, fn = CHUNKS[k]
        came = lax.rem(c + CELLS - j, CELLS)
        return remote(
            x_hbm.at[pl.ds(f0, fn)], first.at[came, pl.ds(f0, fn)],
            z1_send.at[j - 1, k], z1_recv.at[j - 1, k], s, came,
        )

    for k in range(len(CHUNKS)):
        for j in (2, 1, 3):
            send_first(j, k).start()

    def size_of(slot, p):
        return FOOT if PIECES[slot] == 1 else 7 if p < 4 else 6

    def cut(slot, p):
        return pl.ds(6 * p + min(p, 4), size_of(slot, p))

    def halo(slot, p, src, send, sta):
        return remote(src.at[cut(slot, p)], held[slot].at[cut(slot, p)], send, h_recv.at[slot, p], sta, c)

    def halos(slot, src, sta):
        return [halo(slot, p, src, h_send.at[slot, p], sta) for p in range(PIECES[slot])]

    def begin(copies):
        for copy in copies:
            copy.start()

    def to_relay(slot, p, send, sta):
        return remote(
            x_hbm.at[cut(slot, p)], relay.at[pl.ds(0, size_of(slot, p))], send, relay_recv.at[0], sta, c
        )

    def from_relay(slot, p, size, start, sta):
        return remote(
            relay.at[pl.ds(0, size)], held[slot].at[pl.ds(start, size)],
            relay_send.at[0], h_recv.at[slot, p], sta, c,
        )

    def relaying(begins):
        for acts, (slot, source, col, target, direct) in zip(relays, CROSSINGS):
            p = row if direct == 0 else row + 1
            for size, fits in ((7, p < 4), (6, p >= 4)):
                @pl.when(jnp.logical_and(acts, fits))
                def _(slot=slot, source=source, target=target, p=p, size=size):
                    start = 6 * p + (0 if size == 7 else 4)
                    if size == 7:
                        start = 7 * p
                    if begins:
                        to_relay(slot, 0 if size == 7 else 4, h_send.at[BEHIND, 0], beyond + source).wait_recv()
                        from_relay(slot, p, size, start, here + target).start()
                    else:
                        from_relay(slot, p, size, start, here + target).wait_send()

    def table(slot, sta):
        return remote(inv_vmem, tables[slot], t_send.at[slot], t_recv.at[slot], sta, c)

    sent_tables = [
        table(BEHIND, at(2)), table(BESIDE, at(3 - 2 * odd)), table(ASIDE, aside_to), table(FAR, at(8 * odd - 4))
    ]
    begin(sent_tables)
    sent_behind = halos(BEHIND, x_hbm, at(2))
    sent_aside = halos(ASIDE, x_hbm, aside_to)
    sent_far = halos(FAR, held[BEHIND], at(2))
    over_far = [halo(FAR, p, held[ASIDE], over_send.at[p], sibling) for p in range(PIECES[FAR])]
    sent_beside = halos(BESIDE, held[BEHIND], sibling)
    inner = place < 62
    is_odd = odd == 1
    hopping = jnp.logical_and(odd == 0, place >= 4)
    hops = jnp.logical_and(odd == 0, jnp.logical_and(place >= 2, place <= 60))
    sent_hop = [
        remote(x_hbm.at[cut(ASIDE, p)], hop.at[cut(ASIDE, p)], h_send.at[ASIDE, p], hop_recv.at[p], at(-2), c)
        for p in range(PIECES[ASIDE])
    ]
    past_hop = [halo(ASIDE, p, hop, hop_send.at[p], at(-1)) for p in range(PIECES[ASIDE])]

    @pl.when(inner)
    def _():
        begin(sent_behind)

    @pl.when(is_odd)
    def _():
        begin(sent_aside)

    @pl.when(hopping)
    def _():
        begin(sent_hop)

    for slot, source, col, target, direct in CROSSINGS:
        @pl.when(place == source)
        def _(slot=slot, col=col, target=target, direct=direct):
            sends = [cross_send.at[p] if slot == FAR else h_send.at[slot, p] for p in range(8)]
            for p, r in enumerate(relay_rows(direct), 1):
                to_relay(slot, p, sends[p], beyond + r * ROW_STAS + col).start()
            halo(slot, 0, x_hbm, sends[0], beyond + target).start()

    own_first = pltpu.make_async_copy(x_hbm.at[pl.ds(c * PART, PART)], first.at[c], local.at[0])
    own_first.start()
    own_table = pltpu.make_async_copy(inv_vmem, inv_own, local.at[12])
    own_table.start()
    own_held = pltpu.make_async_copy(x_hbm, held[OWN].at[pl.ds(0, FOOT)], local.at[1])
    own_held.start()
    for slot in range(SLOTS):
        held[slot][FOOT] = jnp.zeros((ROWS, WIDTH), BF16)

    for copy in fetched:
        copy.wait()
    kron_rows(sx, wide_x, kx)
    wide = iota((TILES, WIDTH), 1)
    spread = (iota((TILES, WIDTH), 0) == (wide // 128) * TILE + wide % TILE).astype(BF16)
    rows_y = dot(sy[...], spread)
    level = (iota((TILE, WIDTH), 1) // TILE) % 8
    for b in range(4):
        for z in range(8):
            ky[(b * 8 + z) * TILE : (b * 8 + z + 1) * TILE, :] = jnp.where(
                level == z, rows_y[b * TILE : (b + 1) * TILE, :], 0.0
            ).astype(BF16)
    kron_rows(sz, wide_z, wz)

    def smooth_plane(slot, index):
        def along_x(b, carry):
            for x in range(16):
                dense[x * ROWS : (x + 1) * ROWS, :] = held[slot][index(b * 16 + x)]
            mixed = dot(kx[...], dense[...]).astype(BF16)
            for g in range(4):
                across[g, :, pl.ds(pl.multiple_of(b * 128, 128), 128)] = mixed[:, g * 128 : (g + 1) * 128]
            return carry

        lax.fori_loop(0, 4, along_x, 0)

        def along_y(g, carry):
            mixed = dot(across[g], ky[...]).astype(BF16)
            for e in range(4):
                field[
                    e * 16 : (e + 1) * 16, slot * ROWS : (slot + 1) * ROWS, pl.ds(pl.multiple_of(g * 128, 128), 128)
                ] = mixed[:, e * 128 : (e + 1) * 128].reshape(16, ROWS, 128)
            return carry

        lax.fori_loop(0, 4, along_y, 0)

    def take_table(slot):
        copy = pltpu.make_async_copy(tables[slot], inv_smem[slot], local.at[2 + slot])
        copy.start()
        copy.wait()

    own_held.wait()
    own_table.wait()
    smooth_plane(OWN, lambda i: inv_own[0, i])

    def send_second(j, k):
        f0, fn = CHUNKS[k]
        to = lax.rem(c + j, CELLS)
        return remote(
            second.at[to, pl.ds(f0, fn)], smoothed.at[pl.ds(c * PART + f0, fn)],
            z2_send.at[j - 1, k], z2_recv.at[j - 1, k], s, to,
        )

    def recv_second(j, k):
        f0, fn = CHUNKS[k]
        came = lax.rem(c + CELLS - j, CELLS)
        return remote(
            second.at[came, pl.ds(f0, fn)], smoothed.at[pl.ds(came * PART + f0, fn)],
            z2_send.at[j - 1, k], z2_recv.at[j - 1, k], s, came,
        )

    def own_second(k):
        f0, fn = CHUNKS[k]
        return pltpu.make_async_copy(
            second.at[c, pl.ds(f0, fn)], smoothed.at[pl.ds(c * PART + f0, fn)], local.at[7 + k]
        )

    def smooth_depth(k):
        f0, fn = CHUNKS[k]
        for j in (1, 2, 3):
            recv_first(j, k).wait_recv()
        if k == 0:
            own_first.wait()
        rows = jnp.concatenate(
            [first[d, f0 : f0 + fn].reshape(fn * ROWS, WIDTH) for d in range(CELLS)], axis=1
        )
        for j in (2, 1, 3, 0):
            to = lax.rem(c + j, CELLS)
            done = dot(rows, wz[:, pl.ds(pl.multiple_of(to * WIDTH, WIDTH), WIDTH)])
            second[to, f0 : f0 + fn] = done.astype(BF16).reshape(fn, ROWS, WIDTH)
            if j:
                send_second(j, k).start()
            else:
                own_second(k).start()

    @pl.when(hops)
    def _():
        for p in range(PIECES[ASIDE]):
            sent_hop[p].wait_recv()
            past_hop[p].start()

    relaying(True)

    smooth_depth(0)

    onward = jnp.logical_and(inner, is_odd)
    for p in range(PIECES[BEHIND]):
        sent_behind[p].wait_recv()

        @pl.when(onward)
        def _(p=p):
            sent_far[p].start()

    begin(sent_beside)
    sent_tables[0].wait_recv()
    take_table(BEHIND)
    smooth_plane(BEHIND, lambda i: inv_smem[BEHIND][0, i])

    for p in range(PIECES[ASIDE]):
        sent_aside[p].wait_recv()

        @pl.when(is_odd)
        def _(p=p):
            over_far[p].start()

    sent_tables[2].wait_recv()
    take_table(ASIDE)
    smooth_plane(ASIDE, lambda i: inv_smem[ASIDE][0, i])

    smooth_depth(1)

    sent_beside[0].wait_recv()
    sent_tables[1].wait_recv()
    take_table(BESIDE)
    smooth_plane(BESIDE, lambda i: inv_smem[BESIDE][0, i])

    for p in range(PIECES[FAR]):
        sent_far[p].wait_recv()
    sent_tables[3].wait_recv()
    take_table(FAR)
    smooth_plane(FAR, lambda i: inv_smem[FAR][0, i])

    total = jnp.zeros((ROWS, SLOTS * ROWS), F32)
    for k, (f0, fn) in enumerate(CHUNKS):
        own_second(k).wait()
        for j in (1, 2, 3):
            recv_second(j, k).wait_recv()

        def product(e, total, f0=f0, fn=fn):
            for f in range(f0, f0 + fn):
                place = e * PART + f
                total = total + lax.dot_general(
                    smoothed[place], field[lax.rem(foot_own[0, place], 4) * 16 + foot_own[0, place] // 4],
                    (((1,), (1,)), ((), ())), preferred_element_type=F32,
                )
            return total

        total = lax.fori_loop(0, CELLS, product, total)

    square[...] = jnp.zeros((128, 128), F32)
    square[0:ROWS, 0 : SLOTS * ROWS] = total
    flipped = square[...].T
    back = {}
    for i, slot in enumerate((BEHIND, BESIDE, FAR, ASIDE)):
        turned[i] = flipped[slot * ROWS : (slot + 1) * ROWS, :]
    partners = (at(-2), at(-1 - 2 * odd), at(4 - 8 * odd), at(1 + 2 * odd))
    for i in range(4):
        back[i] = remote(turned.at[i], turned_in.at[i], b_send.at[i], b_recv.at[i], partners[i], c)
        back[i].start()
    for i in range(4):
        back[i].wait_recv()

    def mine(slot):
        return total[:, slot * ROWS : (slot + 1) * ROWS]

    def theirs(i):
        return turned_in[i][:, :ROWS]

    beside, aside, far = mine(BESIDE), mine(ASIDE), mine(FAR)
    parts = [
        jnp.where(is_odd, far, theirs(2)),
        jnp.where(is_odd, beside, theirs(3)),
        mine(BEHIND),
        jnp.where(is_odd, theirs(3), beside),
        mine(OWN),
        jnp.where(is_odd, theirs(1), aside),
        theirs(0),
        jnp.where(is_odd, aside, theirs(1)),
        jnp.where(is_odd, theirs(2), far),
    ]
    whole = jnp.concatenate([part * linked[0, j].astype(F32) for j, part in enumerate(parts)], axis=1)
    for e in range(CELLS):
        shares[e, :, 0:SHARE] = whole[:, e * SHARE : (e + 1) * SHARE]
    given = []
    for j in (1, 2, 3):
        to = lax.rem(c + j, CELLS)
        copy = remote(shares.at[to], shares_in.at[j - 1], c_send.at[j - 1], c_recv.at[j - 1], s, to)
        copy.start()
        given.append(copy)
    for copy in given:
        copy.wait_recv()
    out[0] = shares[c] + shares_in[0]
    out[1] = shares_in[1] + shares_in[2]

    for k in range(len(CHUNKS)):
        for j in (1, 2, 3):
            send_first(j, k).wait_send()
            send_second(j, k).wait_send()
    for copy in (*sent_tables, *sent_behind, *sent_aside, *sent_beside, *back.values(), *given):
        copy.wait_send()

    @pl.when(onward)
    def _():
        for copy in sent_far:
            copy.wait_send()

    @pl.when(is_odd)
    def _():
        for copy in over_far:
            copy.wait_send()

    @pl.when(hops)
    def _():
        for copy in past_hop:
            copy.wait_send()

    @pl.when(place == 61)
    def _():
        for p in range(PIECES[FAR]):
            halo(FAR, p, x_hbm, cross_send.at[p], beyond + 1).wait_send()

    relaying(False)


def body(sensitivity, footprint, linked, smooth_x, smooth_y, smooth_z):
    values = jnp.transpose(sensitivity, (1, 0, 2))
    n_k = len(CHUNKS)
    vmem = pl.BlockSpec(memory_space=pltpu.VMEM)
    smem = pl.BlockSpec(memory_space=pltpu.SMEM)
    dma = pltpu.SemaphoreType.DMA
    hbm = pl.BlockSpec(memory_space=pl.ANY)
    shared = pl.pallas_call(
        kernel,
        out_shape=jax.ShapeDtypeStruct((2, ROWS, 128), F32),
        in_specs=[hbm, smem, smem, hbm, hbm, hbm],
        out_specs=vmem,
        scratch_shapes=[
            pltpu.SMEM((8, 128), jnp.int32), pltpu.VMEM((8, 128), jnp.int32),
            pltpu.VMEM((16, 16), BF16), pltpu.VMEM((64, 64), BF16), pltpu.VMEM((128, 128), BF16),
            [pltpu.VMEM((FOOT + 1, ROWS, WIDTH), BF16)] * SLOTS,
            [pltpu.VMEM((8, 128), jnp.int32)] * SLOTS,
            [pltpu.SMEM((8, 128), jnp.int32)] * SLOTS,
            pltpu.VMEM((CELLS, PART, ROWS, WIDTH), BF16),
            pltpu.VMEM((CELLS, PART, ROWS, WIDTH), BF16),
            pltpu.VMEM((FOOT, ROWS, WIDTH), BF16),
            pltpu.VMEM((2048, 2048), BF16),
            pltpu.VMEM((256, 256), BF16),
            pltpu.VMEM((512, 512), BF16),
            pltpu.VMEM((128, 2048), F32),
            pltpu.VMEM((16, 256), F32),
            pltpu.VMEM((256, WIDTH), BF16),
            pltpu.VMEM((4, 256, WIDTH), BF16),
            pltpu.VMEM((TILES, SLOTS * ROWS, WIDTH), BF16),
            pltpu.VMEM((128, 128), F32),
            pltpu.VMEM((4, ROWS, 128), F32),
            pltpu.VMEM((4, ROWS, 128), F32),
            pltpu.VMEM((CELLS, ROWS, 128), F32),
            pltpu.VMEM((CELLS - 1, ROWS, 128), F32),
            dma((3, n_k)), dma((3, n_k)), dma((3, n_k)), dma((3, n_k)),
            dma((SLOTS, 8)), dma((SLOTS, 8)), dma((SLOTS,)), dma((SLOTS,)),
            dma((4,)), dma((4,)), dma((3,)), dma((3,)), dma((13,)),
            pltpu.VMEM((7, ROWS, WIDTH), BF16), dma((8,)), dma((1,)), dma((1,)),
            pltpu.VMEM((FOOT, ROWS, WIDTH), BF16), dma((8,)), dma((8,)), dma((8,)),
        ],
        compiler_params=pltpu.CompilerParams(
            collective_id=0, has_side_effects=True, vmem_limit_bytes=56 * 2**20
        ),
        name="band",
    )(values, footprint, linked, smooth_x, smooth_y, smooth_z)
    return (shared[0] + shared[1])[:, :SHARE]


def solution(mesh):
    return jax.shard_map(
        body,
        mesh=mesh,
        in_specs=(P("sta", None, "cell"), P("sta", None), P("sta", None), P(), P(), P()),
        out_specs=P("sta", "cell"),
        check_vma=False,
    )
```

```python
import jax
import jax.numpy as jnp
from jax import lax
from jax.experimental import pallas as pl
from jax.experimental.pallas import tpu as pltpu
from jax.sharding import PartitionSpec as P

TILE = 16
FOOT = 52
TILES = 64
BAND = 9
ROWS = 16
WIDTH = 512
CELLS = 4
STAS = 128
PART = FOOT // CELLS
CHUNKS = ((0, 8), (8, 5))
SHARE = BAND * ROWS // CELLS
MESH = pl.DeviceIdType.MESH
OWN, BEHIND, BESIDE, ASIDE, FAR = range(5)
SLOTS = 5
F32, BF16 = jnp.float32, jnp.bfloat16
PIECES = {BEHIND: 8, BESIDE: 1, ASIDE: 8, FAR: 8}
ROW_STAS = 8
HALF_STAS = 64


CROSSINGS = (
    (BEHIND, 62, 0, 0, 0), (BEHIND, 63, 1, 1, 0), (FAR, 61, 3, 1, 0), (ASIDE, 0, 4, 61, 7), (ASIDE, 2, 6, 63, 7)
)


def relay_rows(direct):
    return [row for row in range(8) if row != direct]


def iota(shape, dim):
    return lax.broadcasted_iota(jnp.int32, shape, dim)


def dot(a, b):
    return jnp.dot(a, b, preferred_element_type=F32)


def kron_rows(small_ref, wide_ref, big_ref):
    n = small_ref.shape[0]
    repeat = (iota((n, n * TILE), 0) == iota((n, n * TILE), 1) // TILE).astype(BF16)
    wide_ref[...] = dot(small_ref[...], repeat)
    same = iota((TILE, n * TILE), 0) == iota((TILE, n * TILE), 1) % TILE

    def row(a, carry):
        line = jnp.broadcast_to(wide_ref[pl.ds(a, 1), :], (TILE, n * TILE))
        big_ref[pl.ds(pl.multiple_of(a * TILE, TILE), TILE), :] = jnp.where(same, line, 0.0).astype(BF16)
        return carry

    lax.fori_loop(0, n, row, 0)


def kernel(
    x_hbm, foot_own, linked, sx_hbm, sy_hbm, sz_hbm, out,
    inv_own, inv_vmem, sx, sy, sz, held, tables, inv_smem, first, second, smoothed, wz, kx, ky, wide_z, wide_x,
    dense, across, field, square, turned, turned_in, shares, shares_in,
    z1_send, z1_recv, z2_send, z2_recv, h_send, h_recv, t_send, t_recv,
    b_send, b_recv, c_send, c_recv, local, relay, cross_send, relay_send, relay_recv,
    hop, hop_send, hop_recv, over_send,
):
    s = lax.axis_index("sta")
    c = lax.axis_index("cell")
    odd = lax.rem(s, 2)

    def at(distance):
        return lax.rem(s + distance + STAS, STAS)

    def remote(src, dst, send, recv, sta, cell):
        return pltpu.make_async_remote_copy(
            src_ref=src, dst_ref=dst, send_sem=send, recv_sem=recv,
            device_id=(sta, cell), device_id_type=MESH,
        )

    sibling = s + 1 - 2 * odd
    aside_to = at(-3 + 2 * odd)
    place = lax.rem(s, HALF_STAS)
    here = s - place
    beyond = HALF_STAS - here

    fetched = [
        pltpu.make_async_copy(src, dst, local.at[9 + i])
        for i, (src, dst) in enumerate(((sx_hbm, sx), (sy_hbm, sy), (sz_hbm, sz)))
    ]
    for copy in fetched:
        copy.start()
    barrier = pltpu.get_barrier_semaphore()
    for distance in (-4, -3, -2, -1, 1, 2, 3, 4):
        pl.semaphore_signal(barrier, inc=1, device_id=(at(distance), c), device_id_type=MESH)
    for j in (1, 2, 3):
        pl.semaphore_signal(barrier, inc=1, device_id=(s, lax.rem(c + j, CELLS)), device_id_type=MESH)
    row, column = place // ROW_STAS, lax.rem(place, ROW_STAS)
    relays = [jnp.logical_and(column == col, row != direct) for _, _, col, _, direct in CROSSINGS]
    greeted = jnp.int32(11)
    for acts, (slot, source, col, target, direct) in zip(relays, CROSSINGS):
        greeted += jnp.where(acts, 1, 0) + jnp.where(place == source, 7, 0)

        @pl.when(acts)
        def _(source=source):
            pl.semaphore_signal(barrier, inc=1, device_id=(beyond + source, c), device_id_type=MESH)

        @pl.when(place == target)
        def _(col=col, direct=direct):
            for r in relay_rows(direct):
                pl.semaphore_signal(barrier, inc=1, device_id=(here + r * ROW_STAS + col, c), device_id_type=MESH)

    lanes = iota((8, 128), 1)
    tile_at = lax.rem(lanes, 16) * 4 + lanes // 16
    inverse = jnp.full((8, 128), FOOT, jnp.int32)
    for f in range(FOOT):
        inverse = jnp.where(tile_at == foot_own[0, f], f, inverse)
    inv_vmem[...] = inverse

    pl.semaphore_wait(barrier, greeted)

    def send_first(j, k):
        f0, fn = CHUNKS[k]
        to = lax.rem(c + j, CELLS)
        return remote(
            x_hbm.at[pl.ds(to * PART + f0, fn)], first.at[c, pl.ds(f0, fn)],
            z1_send.at[j - 1, k], z1_recv.at[j - 1, k], s, to,
        )

    def recv_first(j, k):
        f0, fn = CHUNKS[k]
        came = lax.rem(c + CELLS - j, CELLS)
        return remote(
            x_hbm.at[pl.ds(f0, fn)], first.at[came, pl.ds(f0, fn)],
            z1_send.at[j - 1, k], z1_recv.at[j - 1, k], s, came,
        )

    for k in range(len(CHUNKS)):
        for j in (2, 1, 3):
            send_first(j, k).start()

    def size_of(slot, p):
        return FOOT if PIECES[slot] == 1 else 7 if p < 4 else 6

    def cut(slot, p):
        return pl.ds(6 * p + min(p, 4), size_of(slot, p))

    def halo(slot, p, src, send, sta):
        return remote(src.at[cut(slot, p)], held[slot].at[cut(slot, p)], send, h_recv.at[slot, p], sta, c)

    def halos(slot, src, sta):
        return [halo(slot, p, src, h_send.at[slot, p], sta) for p in range(PIECES[slot])]

    def begin(copies):
        for copy in copies:
            copy.start()

    def to_relay(slot, p, send, sta):
        return remote(
            x_hbm.at[cut(slot, p)], relay.at[pl.ds(0, size_of(slot, p))], send, relay_recv.at[0], sta, c
        )

    def from_relay(slot, p, size, start, sta):
        return remote(
            relay.at[pl.ds(0, size)], held[slot].at[pl.ds(start, size)],
            relay_send.at[0], h_recv.at[slot, p], sta, c,
        )

    def relaying(begins):
        for acts, (slot, source, col, target, direct) in zip(relays, CROSSINGS):
            p = row if direct == 0 else row + 1
            for size, fits in ((7, p < 4), (6, p >= 4)):
                @pl.when(jnp.logical_and(acts, fits))
                def _(slot=slot, source=source, target=target, p=p, size=size):
                    start = 6 * p + (0 if size == 7 else 4)
                    if size == 7:
                        start = 7 * p
                    if begins:
                        to_relay(slot, 0 if size == 7 else 4, h_send.at[BEHIND, 0], beyond + source).wait_recv()
                        from_relay(slot, p, size, start, here + target).start()
                    else:
                        from_relay(slot, p, size, start, here + target).wait_send()

    def table(slot, sta):
        return remote(inv_vmem, tables[slot], t_send.at[slot], t_recv.at[slot], sta, c)

    sent_tables = [
        table(BEHIND, at(2)), table(BESIDE, at(3 - 2 * odd)), table(ASIDE, aside_to), table(FAR, at(8 * odd - 4))
    ]
    begin(sent_tables)
    sent_behind = halos(BEHIND, x_hbm, at(2))
    sent_aside = halos(ASIDE, x_hbm, aside_to)
    sent_far = halos(FAR, held[BEHIND], at(2))
    over_far = [halo(FAR, p, held[ASIDE], over_send.at[p], sibling) for p in range(PIECES[FAR])]
    sent_beside = halos(BESIDE, held[BEHIND], sibling)
    inner = place < 62
    is_odd = odd == 1
    hopping = jnp.logical_and(odd == 0, place >= 4)
    hops = jnp.logical_and(odd == 0, jnp.logical_and(place >= 2, place <= 60))
    sent_hop = [
        remote(x_hbm.at[cut(ASIDE, p)], hop.at[cut(ASIDE, p)], h_send.at[ASIDE, p], hop_recv.at[p], at(-2), c)
        for p in range(PIECES[ASIDE])
    ]
    past_hop = [halo(ASIDE, p, hop, hop_send.at[p], at(-1)) for p in range(PIECES[ASIDE])]

    @pl.when(inner)
    def _():
        begin(sent_behind)

    @pl.when(is_odd)
    def _():
        begin(sent_aside)

    @pl.when(hopping)
    def _():
        begin(sent_hop)

    for slot, source, col, target, direct in CROSSINGS:
        @pl.when(place == source)
        def _(slot=slot, col=col, target=target, direct=direct):
            sends = [cross_send.at[p] if slot == FAR else h_send.at[slot, p] for p in range(8)]
            for p, r in enumerate(relay_rows(direct), 1):
                to_relay(slot, p, sends[p], beyond + r * ROW_STAS + col).start()
            halo(slot, 0, x_hbm, sends[0], beyond + target).start()

    own_first = pltpu.make_async_copy(x_hbm.at[pl.ds(c * PART, PART)], first.at[c], local.at[0])
    own_first.start()
    own_table = pltpu.make_async_copy(inv_vmem, inv_own, local.at[12])
    own_table.start()
    own_held = pltpu.make_async_copy(x_hbm, held[OWN].at[pl.ds(0, FOOT)], local.at[1])
    own_held.start()
    for slot in range(SLOTS):
        held[slot][FOOT] = jnp.zeros((ROWS, WIDTH), BF16)

    for copy in fetched:
        copy.wait()
    kron_rows(sx, wide_x, kx)
    wide = iota((TILES, WIDTH), 1)
    spread = (iota((TILES, WIDTH), 0) == (wide // 128) * TILE + wide % TILE).astype(BF16)
    rows_y = dot(sy[...], spread)
    level = (iota((TILE, WIDTH), 1) // TILE) % 8
    for b in range(4):
        for z in range(8):
            ky[(b * 8 + z) * TILE : (b * 8 + z + 1) * TILE, :] = jnp.where(
                level == z, rows_y[b * TILE : (b + 1) * TILE, :], 0.0
            ).astype(BF16)
    kron_rows(sz, wide_z, wz)

    def smooth_plane(slot, index):
        def along_x(b, carry):
            for x in range(16):
                dense[x * ROWS : (x + 1) * ROWS, :] = held[slot][index(b * 16 + x)]
            mixed = dot(kx[...], dense[...]).astype(BF16)
            for g in range(4):
                across[g, :, pl.ds(pl.multiple_of(b * 128, 128), 128)] = mixed[:, g * 128 : (g + 1) * 128]
            return carry

        lax.fori_loop(0, 4, along_x, 0)

        def along_y(g, carry):
            mixed = dot(across[g], ky[...]).astype(BF16)
            for e in range(4):
                field[
                    e * 16 : (e + 1) * 16, slot * ROWS : (slot + 1) * ROWS, pl.ds(pl.multiple_of(g * 128, 128), 128)
                ] = mixed[:, e * 128 : (e + 1) * 128].reshape(16, ROWS, 128)
            return carry

        lax.fori_loop(0, 4, along_y, 0)

    def take_table(slot):
        copy = pltpu.make_async_copy(tables[slot], inv_smem[slot], local.at[2 + slot])
        copy.start()
        copy.wait()

    own_held.wait()
    own_table.wait()
    smooth_plane(OWN, lambda i: inv_own[0, i])

    def send_second(j, k):
        f0, fn = CHUNKS[k]
        to = lax.rem(c + j, CELLS)
        return remote(
            second.at[to, pl.ds(f0, fn)], smoothed.at[pl.ds(c * PART + f0, fn)],
            z2_send.at[j - 1, k], z2_recv.at[j - 1, k], s, to,
        )

    def recv_second(j, k):
        f0, fn = CHUNKS[k]
        came = lax.rem(c + CELLS - j, CELLS)
        return remote(
            second.at[came, pl.ds(f0, fn)], smoothed.at[pl.ds(came * PART + f0, fn)],
            z2_send.at[j - 1, k], z2_recv.at[j - 1, k], s, came,
        )

    def own_second(k):
        f0, fn = CHUNKS[k]
        return pltpu.make_async_copy(
            second.at[c, pl.ds(f0, fn)], smoothed.at[pl.ds(c * PART + f0, fn)], local.at[7 + k]
        )

    def smooth_depth(k):
        f0, fn = CHUNKS[k]
        for j in (1, 2, 3):
            recv_first(j, k).wait_recv()
        if k == 0:
            own_first.wait()
        rows = jnp.concatenate(
            [first[d, f0 : f0 + fn].reshape(fn * ROWS, WIDTH) for d in range(CELLS)], axis=1
        )
        for j in (2, 1, 3, 0):
            to = lax.rem(c + j, CELLS)
            done = dot(rows, wz[:, pl.ds(pl.multiple_of(to * WIDTH, WIDTH), WIDTH)])
            second[to, f0 : f0 + fn] = done.astype(BF16).reshape(fn, ROWS, WIDTH)
            if j:
                send_second(j, k).start()
            else:
                own_second(k).start()

    @pl.when(hops)
    def _():
        for p in range(PIECES[ASIDE]):
            sent_hop[p].wait_recv()
            past_hop[p].start()

    relaying(True)

    smooth_depth(0)

    onward = jnp.logical_and(inner, is_odd)
    for p in range(PIECES[BEHIND]):
        sent_behind[p].wait_recv()

        @pl.when(onward)
        def _(p=p):
            sent_far[p].start()

    begin(sent_beside)
    sent_tables[0].wait_recv()
    take_table(BEHIND)
    smooth_plane(BEHIND, lambda i: inv_smem[BEHIND][0, i])

    for p in range(PIECES[ASIDE]):
        sent_aside[p].wait_recv()

        @pl.when(is_odd)
        def _(p=p):
            over_far[p].start()

    sent_tables[2].wait_recv()
    take_table(ASIDE)
    smooth_plane(ASIDE, lambda i: inv_smem[ASIDE][0, i])

    smooth_depth(1)

    sent_beside[0].wait_recv()
    sent_tables[1].wait_recv()
    take_table(BESIDE)
    smooth_plane(BESIDE, lambda i: inv_smem[BESIDE][0, i])

    for p in range(PIECES[FAR]):
        sent_far[p].wait_recv()
    sent_tables[3].wait_recv()
    take_table(FAR)
    smooth_plane(FAR, lambda i: inv_smem[FAR][0, i])

    total = jnp.zeros((ROWS, SLOTS * ROWS), F32)
    for k, (f0, fn) in enumerate(CHUNKS):
        own_second(k).wait()
        for j in (1, 2, 3):
            recv_second(j, k).wait_recv()

        def product(e, total, f0=f0, fn=fn):
            for f in range(f0, f0 + fn):
                place = e * PART + f
                total = total + lax.dot_general(
                    smoothed[place], field[lax.rem(foot_own[0, place], 4) * 16 + foot_own[0, place] // 4],
                    (((1,), (1,)), ((), ())), preferred_element_type=F32,
                )
            return total

        total = lax.fori_loop(0, CELLS, product, total)

    square[...] = jnp.zeros((128, 128), F32)
    square[0:ROWS, 0 : SLOTS * ROWS] = total
    flipped = square[...].T
    back = {}
    for i, slot in enumerate((BEHIND, BESIDE, FAR, ASIDE)):
        turned[i] = flipped[slot * ROWS : (slot + 1) * ROWS, :]
    partners = (at(-2), at(-1 - 2 * odd), at(4 - 8 * odd), at(1 + 2 * odd))
    for i in range(4):
        back[i] = remote(turned.at[i], turned_in.at[i], b_send.at[i], b_recv.at[i], partners[i], c)
        back[i].start()
    for i in range(4):
        back[i].wait_recv()

    def mine(slot):
        return total[:, slot * ROWS : (slot + 1) * ROWS]

    def theirs(i):
        return turned_in[i][:, :ROWS]

    beside, aside, far = mine(BESIDE), mine(ASIDE), mine(FAR)
    parts = [
        jnp.where(is_odd, far, theirs(2)),
        jnp.where(is_odd, beside, theirs(3)),
        mine(BEHIND),
        jnp.where(is_odd, theirs(3), beside),
        mine(OWN),
        jnp.where(is_odd, theirs(1), aside),
        theirs(0),
        jnp.where(is_odd, aside, theirs(1)),
        jnp.where(is_odd, theirs(2), far),
    ]
    whole = jnp.concatenate([part * linked[0, j].astype(F32) for j, part in enumerate(parts)], axis=1)
    for e in range(CELLS):
        shares[e, :, 0:SHARE] = whole[:, e * SHARE : (e + 1) * SHARE]
    given = []
    for j in (1, 2, 3):
        to = lax.rem(c + j, CELLS)
        copy = remote(shares.at[to], shares_in.at[j - 1], c_send.at[j - 1], c_recv.at[j - 1], s, to)
        copy.start()
        given.append(copy)
    for copy in given:
        copy.wait_recv()
    out[0] = shares[c] + shares_in[0]
    out[1] = shares_in[1] + shares_in[2]

    for k in range(len(CHUNKS)):
        for j in (1, 2, 3):
            send_first(j, k).wait_send()
            send_second(j, k).wait_send()
    for copy in (*sent_tables, *sent_behind, *sent_aside, *sent_beside, *back.values(), *given):
        copy.wait_send()

    @pl.when(onward)
    def _():
        for copy in sent_far:
            copy.wait_send()

    @pl.when(is_odd)
    def _():
        for copy in over_far:
            copy.wait_send()

    @pl.when(hops)
    def _():
        for copy in past_hop:
            copy.wait_send()

    @pl.when(place == 61)
    def _():
        for p in range(PIECES[FAR]):
            halo(FAR, p, x_hbm, cross_send.at[p], beyond + 1).wait_send()

    relaying(False)


def body(sensitivity, footprint, linked, smooth_x, smooth_y, smooth_z):
    values = jnp.transpose(sensitivity, (1, 0, 2))
    n_k = len(CHUNKS)
    vmem = pl.BlockSpec(memory_space=pltpu.VMEM)
    smem = pl.BlockSpec(memory_space=pltpu.SMEM)
    dma = pltpu.SemaphoreType.DMA
    hbm = pl.BlockSpec(memory_space=pl.ANY)
    shared = pl.pallas_call(
        kernel,
        out_shape=jax.ShapeDtypeStruct((2, ROWS, 128), F32),
        in_specs=[hbm, smem, smem, hbm, hbm, hbm],
        out_specs=vmem,
        scratch_shapes=[
            pltpu.SMEM((8, 128), jnp.int32), pltpu.VMEM((8, 128), jnp.int32),
            pltpu.VMEM((16, 16), BF16), pltpu.VMEM((64, 64), BF16), pltpu.VMEM((128, 128), BF16),
            [pltpu.VMEM((FOOT + 1, ROWS, WIDTH), BF16)] * SLOTS,
            [pltpu.VMEM((8, 128), jnp.int32)] * SLOTS,
            [pltpu.SMEM((8, 128), jnp.int32)] * SLOTS,
            pltpu.VMEM((CELLS, PART, ROWS, WIDTH), BF16),
            pltpu.VMEM((CELLS, PART, ROWS, WIDTH), BF16),
            pltpu.VMEM((FOOT, ROWS, WIDTH), BF16),
            pltpu.VMEM((2048, 2048), BF16),
            pltpu.VMEM((256, 256), BF16),
            pltpu.VMEM((512, 512), BF16),
            pltpu.VMEM((128, 2048), F32),
            pltpu.VMEM((16, 256), F32),
            pltpu.VMEM((256, WIDTH), BF16),
            pltpu.VMEM((4, 256, WIDTH), BF16),
            pltpu.VMEM((TILES, SLOTS * ROWS, WIDTH), BF16),
            pltpu.VMEM((128, 128), F32),
            pltpu.VMEM((4, ROWS, 128), F32),
            pltpu.VMEM((4, ROWS, 128), F32),
            pltpu.VMEM((CELLS, ROWS, 128), F32),
            pltpu.VMEM((CELLS - 1, ROWS, 128), F32),
            dma((3, n_k)), dma((3, n_k)), dma((3, n_k)), dma((3, n_k)),
            dma((SLOTS, 8)), dma((SLOTS, 8)), dma((SLOTS,)), dma((SLOTS,)),
            dma((4,)), dma((4,)), dma((3,)), dma((3,)), dma((13,)),
            pltpu.VMEM((7, ROWS, WIDTH), BF16), dma((8,)), dma((1,)), dma((1,)),
            pltpu.VMEM((FOOT, ROWS, WIDTH), BF16), dma((8,)), dma((8,)), dma((8,)),
        ],
        compiler_params=pltpu.CompilerParams(
            collective_id=0, has_side_effects=True, vmem_limit_bytes=56 * 2**20
        ),
        name="band",
    )(values, footprint, linked, smooth_x, smooth_y, smooth_z)
    return (shared[0] + shared[1])[:, :SHARE]


def solution(mesh):
    return jax.shard_map(
        body,
        mesh=mesh,
        in_specs=(P("sta", None, "cell"), P("sta", None), P("sta", None), P(), P(), P()),
        out_specs=P("sta", "cell"),
        check_vma=False,
    )
```
